128 devices in a mesh: inp: 8 (over z, x_hi), tm: 8 (over x_lo, y), bl: 2 (over core).
Axes of the slice: x: 4 (x_hi: 2, x_lo: 2; x = x_hi * 2 + x_lo), y: 4, z: 4, core: 2. Of those that a mesh axis runs over, the one named last changes fastest.
Arguments:
- voltages: int32 [1024, 524288], P(('inp', 'bl'), 'tm'), may hold values from -16 to 14, as said below
- taps: float32 [4, 16384], replicated, may hold values from -3 to 3
- flags: int32 [1024], P(('inp', 'bl')), may hold values 0 or 1
Outputs:
- visibilities: float32 [2, 128, 8, 128, 1024], P(None, ('inp', 'tm'), None, 'bl')
The draws below stay inside these ranges and needn't reach their ends.
Inputs may be any that keep to these rules, and one draw needn't show every extreme that they name: `voltages`: int8-valued digitized samples, each input's stream in time order.
All inputs are finite; a program needn't handle non-finite values. No bound on the sum of `flags` on one device may be relied on, other than what follows from the above.
Results may differ from the reference program's by a relative error of at most 0.00065.
Values may be sent and summed in bfloat16 or wider, within the bound.
A program may use at most 192 MiB of HBM per device.

```python
import math
import jax
import jax.numpy as jnp
from jax import lax

NI = 1024
NCH = 8192
TAPS = 4
CH_AVG = 64
SPECTRA = 32
SAMPLES = 524288
NOUT = 128
N_INP = 8


def draw_voltages(key, part):
    base = jax.random.fold_in(key, 17)
    key_shared, key_private = jax.random.split(base)
    shared = jax.random.randint(key_shared, (1, SAMPLES), -8, 8, dtype=jnp.int32)
    private = jax.random.randint(key_private, (NI, SAMPLES), -8, 8, dtype=jnp.int32)
    return shared + private


def place_ends(drawn, rng, smallest, top_value):
    longest = drawn.shape.index(max(drawn.shape))
    spots = []
    for shift in (0, 1):
        where = [jax.random.randint(jax.random.fold_in(rng, axis), (), 0, length) for axis, length in enumerate(drawn.shape)]
        where[longest] = (where[longest] + shift) % drawn.shape[longest]
        spots.append(tuple(where))
    return drawn.at[spots[0]].set(smallest).at[spots[1]].set(top_value)


def gaussian(own_key, shape, spread, most, kind=jnp.bfloat16):
    return jnp.clip(spread * jax.random.normal(own_key, shape, jnp.float32), -most, most).astype(kind)


def setup_inputs(seed: int = 0) -> dict:
    arg_keys = jax.random.split(jax.random.key(seed), 4)
    voltages = draw_voltages(jax.random.fold_in(arg_keys[3], 71), 0)
    taps = gaussian(arg_keys[1], (TAPS, 2 * NCH), 0.5, 3.0, jnp.float32)
    flags = place_ends((jax.random.randint(arg_keys[2], (NI,), 0, 8) < 7).astype(jnp.int32), jax.random.fold_in(arg_keys[2], 1), 0, 1)
    return {"voltages": voltages, "taps": taps, "flags": flags}


def reference(voltages, taps, flags):
    length = 2 * NCH
    block_inputs = math.gcd(NI, 64)
    block_count = NI // block_inputs
    blocked = voltages.reshape(block_count, block_inputs, SPECTRA, length)
    flag_blocks = flags.reshape(block_count, block_inputs)

    def filter_section(packed):
        raw_block, flag_block = packed
        samples = raw_block.astype(jnp.float32)
        padded = jnp.concatenate([samples, jnp.zeros((block_inputs, TAPS - 1, length), jnp.float32)], axis=1)
        filtered = jnp.zeros((block_inputs, SPECTRA, length), jnp.float32)
        for offset in range(TAPS):
            filtered = filtered + taps[offset][None, None, :] * padded[:, offset:offset + SPECTRA]
        transformed = jnp.fft.rfft(filtered, axis=-1)[..., :NCH]
        scale = flag_block.astype(jnp.float32)[:, None, None] / (8.0 * math.sqrt(length))
        stacked = jnp.stack([jnp.real(transformed) * scale, jnp.imag(transformed) * scale])
        return stacked.astype(jnp.bfloat16)
    spectra = lax.map(filter_section, (blocked, flag_blocks))
    spectra = jnp.transpose(spectra, (1, 0, 2, 3, 4)).reshape(2, NI, SPECTRA, NCH)
    norm = 1.0 / (SPECTRA * CH_AVG)
    highest = lax.Precision.HIGHEST

    def cross_section(group):
        start = (group * CH_AVG).astype(jnp.int32)
        segment = lax.dynamic_slice_in_dim(spectra, start, CH_AVG, 3).astype(jnp.float32)
        segment = segment.reshape(2, NI, SPECTRA * CH_AVG)
        real_rows = segment[0]
        imag_rows = segment[1]
        real_vis = jnp.dot(real_rows, real_rows.T, precision=highest) + jnp.dot(imag_rows, imag_rows.T, precision=highest)
        imag_vis = jnp.dot(imag_rows, real_rows.T, precision=highest) - jnp.dot(real_rows, imag_rows.T, precision=highest)
        return jnp.stack([real_vis, imag_vis]) * norm
    visibilities = lax.map(cross_section, jnp.arange(NOUT, dtype=jnp.int32))
    visibilities = jnp.transpose(visibilities, (1, 0, 2, 3))
    return visibilities.reshape(2, NOUT, N_INP, NI // N_INP, NI)
```

```python
import math

import jax
import jax.numpy as jnp
from jax import lax
from jax.sharding import PartitionSpec as P

CH_AVG = 64
FIRST = 128


def passed_along(value, axis, steps):
    count = lax.axis_size(axis)
    initial, last = (max(0, -steps), min(count, count - steps))
    return lax.ppermute(value, axis, [(source, source + steps) for source in range(initial, last)])


def cos_sin(height, breadth, period):
    grid = lax.broadcasted_iota(jnp.int32, (height, breadth), 0) * lax.broadcasted_iota(
        jnp.int32, (height, breadth), 1
    )
    angle = (grid % period).astype(jnp.float32) * (2.0 * math.pi / period)
    return (jnp.cos(angle), jnp.sin(angle))


def transform(blocks, length, precision):
    first_len = FIRST
    second_len = length // first_len
    highs = length // 2 // first_len
    cos_one, sin_one = cos_sin(first_len, first_len, first_len)
    table_one = jnp.stack([cos_one, -sin_one])
    section_one = jnp.einsum("xca,mab->xmcb", table_one, blocks, precision=precision)
    cos_twist, sin_twist = cos_sin(first_len, second_len, length)
    real_one = section_one[0]
    imag_one = section_one[1]
    twisted = jnp.stack(
        [real_one * cos_twist + imag_one * sin_twist, imag_one * cos_twist - real_one * sin_twist]
    )
    cos_two, sin_two = cos_sin(highs, second_len, second_len)
    table_two = jnp.stack(
        [jnp.stack([cos_two, sin_two], axis=1), jnp.stack([-sin_two, cos_two], axis=1)]
    )
    return jnp.einsum("yqxb,xmcb->yqmc", table_two, twisted, precision=precision)


def shards(voltages, taps, flags):
    inputs = voltages.shape[0]
    tap_count = taps.shape[0]
    length = taps.shape[1]
    spectra_dev = voltages.shape[1] // length
    reach = tap_count - 1
    samples = voltages.astype(jnp.float32).reshape(inputs, spectra_dev, length)
    leading = voltages[:, : reach * length].reshape(inputs, reach, length).astype(jnp.bfloat16)
    following = passed_along(leading, "tm", -1)
    extended = jnp.concatenate([samples, following.astype(jnp.float32)], axis=1)
    filtered = jnp.zeros((inputs, spectra_dev, length), jnp.float32)
    for offset in range(tap_count):
        filtered = (
            filtered + taps[offset][None, None, :] * extended[:, offset : offset + spectra_dev]
        )
    blocks = filtered.reshape(inputs * spectra_dev, FIRST, length // FIRST)
    both_parts = transform(blocks, length, lax.Precision.HIGHEST)
    scale = jnp.repeat(flags.astype(jnp.float32) / (8.0 * math.sqrt(length)), spectra_dev)
    spectra = (both_parts * scale[None, None, :, None]).astype(jnp.bfloat16)
    turned = lax.all_to_all(spectra, ("inp", "tm"), split_axis=1, concat_axis=1, tiled=True)
    groups_inp = lax.axis_size("inp")
    groups_tm = lax.axis_size("tm")
    out_groups = FIRST // CH_AVG
    rows = turned.reshape(2, groups_inp, groups_tm, inputs, spectra_dev, out_groups, CH_AVG)
    own = jnp.transpose(rows, (5, 1, 3, 0, 2, 4, 6)).reshape(out_groups, groups_inp, inputs, -1)
    half = own.shape[-1] // 2
    swapped = jnp.concatenate([own[..., half:], -own[..., :half]], axis=-1)
    lhs = jnp.stack([own, swapped], axis=1).reshape(out_groups, 2, groups_inp * inputs, -1)
    columns = lax.all_gather(own, "bl", axis=2, tiled=True).reshape(out_groups, -1, 2 * half)
    count = float(groups_tm * spectra_dev * CH_AVG)
    products = jnp.einsum("gxpk,gqk->xgpq", lhs, columns, preferred_element_type=jnp.float32)
    visibilities = products * (1.0 / count)
    return visibilities.reshape(2, out_groups, groups_inp, inputs, columns.shape[1])


def solution(mesh):
    in_specs = (P(("inp", "bl"), "tm"), P(), P(("inp", "bl")))
    out_specs = P(None, ("inp", "tm"), None, "bl", None)
    return jax.shard_map(shards, mesh=mesh, in_specs=in_specs, out_specs=out_specs, check_vma=False)
```

```python
import math

import jax
import jax.numpy as jnp
from jax import lax
from jax.sharding import PartitionSpec as P

CH_AVG = 64
FIRST = 128


def passed_along(value, axis, steps):
    count = lax.axis_size(axis)
    initial, last = (max(0, -steps), min(count, count - steps))
    return lax.ppermute(value, axis, [(source, source + steps) for source in range(initial, last)])


def cos_sin(height, breadth, period):
    grid = lax.broadcasted_iota(jnp.int32, (height, breadth), 0) * lax.broadcasted_iota(
        jnp.int32, (height, breadth), 1
    )
    angle = (grid % period).astype(jnp.float32) * (2.0 * math.pi / period)
    return (jnp.cos(angle), jnp.sin(angle))


def transform(blocks, length, precision):
    first_len = FIRST
    second_len = length // first_len
    highs = length // 2 // first_len
    cos_one, sin_one = cos_sin(first_len, first_len, first_len)
    table_one = jnp.stack([cos_one, -sin_one])
    section_one = jnp.einsum("xca,mab->xmcb", table_one, blocks, precision=precision)
    cos_twist, sin_twist = cos_sin(first_len, second_len, length)
    real_one = section_one[0]
    imag_one = section_one[1]
    twisted = jnp.stack(
        [real_one * cos_twist + imag_one * sin_twist, imag_one * cos_twist - real_one * sin_twist]
    )
    cos_two, sin_two = cos_sin(highs, second_len, second_len)
    table_two = jnp.stack(
        [jnp.stack([cos_two, sin_two], axis=1), jnp.stack([-sin_two, cos_two], axis=1)]
    )
    return jnp.einsum("yqxb,xmcb->yqmc", table_two, twisted, precision=precision)


def shards(voltages, taps, flags):
    inputs = voltages.shape[0]
    tap_count = taps.shape[0]
    length = taps.shape[1]
    spectra_dev = voltages.shape[1] // length
    reach = tap_count - 1
    samples = voltages.astype(jnp.float32).reshape(inputs, spectra_dev, length)
    leading = voltages[:, : reach * length].reshape(inputs, reach, length).astype(jnp.bfloat16)
    following = passed_along(leading, "tm", -1)
    extended = jnp.concatenate([samples, following.astype(jnp.float32)], axis=1)

    def filtered(source, first, count):
        total = jnp.zeros((inputs, count, length), jnp.float32)
        for offset in range(tap_count):
            start = first + offset
            total = total + taps[offset][None, None, :] * source[:, start : start + count]
        return total.reshape(inputs * count, FIRST, length // FIRST)

    local = spectra_dev - reach
    parts = [transform(filtered(samples, 0, local), length, lax.Precision.HIGH)]
    parts.append(transform(filtered(extended, local, reach), length, lax.Precision.HIGH))
    highs = parts[0].shape[1]
    both_parts = jnp.concatenate(
        [parts[0].reshape(2, highs, inputs, local, FIRST), parts[1].reshape(2, highs, inputs, reach, FIRST)],
        axis=3,
    ).reshape(2, highs, inputs * spectra_dev, FIRST)
    scale = jnp.repeat(flags.astype(jnp.float32) / (8.0 * math.sqrt(length)), spectra_dev)
    spectra = both_parts * scale[None, None, :, None]
    out_groups = FIRST // CH_AVG
    spectra = spectra.reshape(2, highs, inputs, spectra_dev, out_groups, CH_AVG)
    spectra = jnp.transpose(spectra, (1, 4, 2, 0, 3, 5)).reshape(highs, out_groups, inputs, -1)
    spectra = spectra.astype(jnp.bfloat16)
    turned = lax.all_to_all(spectra, ("inp", "tm"), split_axis=0, concat_axis=0, tiled=True)
    groups_inp = lax.axis_size("inp")
    groups_tm = lax.axis_size("tm")
    own = turned.reshape(groups_inp, groups_tm, out_groups, inputs, -1)
    half = own.shape[-1] // 2
    swapped = jnp.concatenate([own[..., half:], -own[..., :half]], axis=-1)
    lhs = jnp.stack([own, swapped])
    columns = lax.all_gather(own, "bl", axis=3, tiled=True)
    count = float(groups_tm * spectra_dev * CH_AVG)
    products = jnp.einsum("xptgik,qtgjk->xgpiqj", lhs, columns, preferred_element_type=jnp.float32)
    visibilities = products * (1.0 / count)
    return visibilities.reshape(2, out_groups, groups_inp, inputs, -1)


def solution(mesh):
    in_specs = (P(("inp", "bl"), "tm"), P(), P(("inp", "bl")))
    out_specs = P(None, ("inp", "tm"), None, "bl", None)
    return jax.shard_map(shards, mesh=mesh, in_specs=in_specs, out_specs=out_specs, check_vma=False)
```

```python
import math

import jax
import jax.numpy as jnp
from jax import lax
from jax.sharding import PartitionSpec as P

CH_AVG = 64
FIRST = 128


def passed_along(value, axis, steps):
    count = lax.axis_size(axis)
    initial, last = (max(0, -steps), min(count, count - steps))
    return lax.ppermute(value, axis, [(source, source + steps) for source in range(initial, last)])


def cos_sin(height, breadth, period):
    grid = lax.broadcasted_iota(jnp.int32, (height, breadth), 0) * lax.broadcasted_iota(
        jnp.int32, (height, breadth), 1
    )
    angle = (grid % period).astype(jnp.float32) * (2.0 * math.pi / period)
    return (jnp.cos(angle), jnp.sin(angle))


def transform(blocks, length, precision):
    first_len = FIRST
    second_len = length // first_len
    highs = length // 2 // first_len
    cos_one, sin_one = cos_sin(first_len, first_len, first_len)
    table_one = jnp.stack([cos_one, -sin_one])
    section_one = jnp.einsum("xca,mab->xmcb", table_one, blocks, precision=precision)
    cos_twist, sin_twist = cos_sin(first_len, second_len, length)
    real_one = section_one[0]
    imag_one = section_one[1]
    twisted = jnp.stack(
        [real_one * cos_twist + imag_one * sin_twist, imag_one * cos_twist - real_one * sin_twist]
    )
    cos_two, sin_two = cos_sin(highs, second_len, second_len)
    table_two = jnp.stack(
        [jnp.stack([cos_two, sin_two], axis=1), jnp.stack([-sin_two, cos_two], axis=1)]
    )
    return jnp.einsum("yqxb,xmcb->yqmc", table_two, twisted, precision=precision)


def shards(voltages, taps, flags):
    inputs = voltages.shape[0]
    tap_count = taps.shape[0]
    length = taps.shape[1]
    second_len = length // FIRST
    spectra_dev = voltages.shape[1] // length
    reach = tap_count - 1
    local = spectra_dev - reach
    precision = lax.Precision.HIGH
    blocked = voltages.reshape(inputs, spectra_dev, FIRST, second_len)
    leading = blocked[:, :reach].astype(jnp.bfloat16)
    following = passed_along(leading, "tm", -1)
    samples = blocked.astype(jnp.float32)
    tap_blocks = taps.reshape(tap_count, FIRST, second_len)

    def filtered(pieces, count):
        rows = []
        for spectrum in range(count):
            total = jnp.zeros((inputs, FIRST, second_len), jnp.float32)
            for offset in range(tap_count):
                total = total + tap_blocks[offset][None] * pieces[spectrum + offset]
            rows.append(total)
        return jnp.concatenate(rows, axis=0)

    own_pieces = [samples[:, j] for j in range(spectra_dev)]
    next_pieces = [following[:, j].astype(jnp.float32) for j in range(reach)]
    first_part = transform(filtered(own_pieces, local), length, precision)
    second_part = transform(filtered(own_pieces[local:] + next_pieces, reach), length, precision)
    both_parts = jnp.concatenate([first_part, second_part], axis=2)
    scale = jnp.tile(flags.astype(jnp.float32) / (8.0 * math.sqrt(length)), spectra_dev)
    spectra = (both_parts * scale[None, None, :, None]).astype(jnp.bfloat16)
    turned = lax.all_to_all(spectra, ("inp", "tm"), split_axis=1, concat_axis=1, tiled=True)
    groups_inp = lax.axis_size("inp")
    groups_tm = lax.axis_size("tm")
    out_groups = FIRST // CH_AVG
    rows = turned.reshape(2, groups_inp, groups_tm, spectra_dev, inputs, FIRST)
    own = jnp.transpose(rows, (1, 4, 0, 2, 3, 5)).reshape(groups_inp, inputs, -1)
    half = own.shape[-1] // 2
    swapped = jnp.concatenate([own[..., half:], -own[..., :half]], axis=-1)
    lane_group = (lax.broadcasted_iota(jnp.int32, (out_groups, own.shape[-1]), 1) % FIRST) // CH_AVG
    mask = (lane_group == lax.broadcasted_iota(jnp.int32, (out_groups, own.shape[-1]), 0))
    mask = mask.astype(own.dtype)
    lhs = jnp.stack([own, swapped])[:, None] * mask[None, :, None, None, :]
    columns = lax.all_gather(own, "bl", axis=1, tiled=True).reshape(-1, own.shape[-1])
    count = float(groups_tm * spectra_dev * CH_AVG)
    products = jnp.einsum("xgpik,qk->xgpiq", lhs, columns, preferred_element_type=jnp.float32)
    return products * (1.0 / count)


def solution(mesh):
    in_specs = (P(("inp", "bl"), "tm"), P(), P(("inp", "bl")))
    out_specs = P(None, ("inp", "tm"), None, "bl", None)
    return jax.shard_map(shards, mesh=mesh, in_specs=in_specs, out_specs=out_specs, check_vma=False)
```

```python
import math

import jax
import jax.numpy as jnp
from jax import lax
from jax.experimental import pallas as pl
from jax.experimental.pallas import tpu as pltpu
from jax.sharding import PartitionSpec as P

CH_AVG = 64
FIRST = 128


def passed_along(value, axis, steps):
    count = lax.axis_size(axis)
    initial, last = (max(0, -steps), min(count, count - steps))
    return lax.ppermute(value, axis, [(source, source + steps) for source in range(initial, last)])


def cos_sin(height, breadth, period):
    grid = lax.broadcasted_iota(jnp.int32, (height, breadth), 0) * lax.broadcasted_iota(
        jnp.int32, (height, breadth), 1
    )
    angle = (grid % period).astype(jnp.float32) * (2.0 * math.pi / period)
    return (jnp.cos(angle), jnp.sin(angle))


def transform(blocks, length, precision):
    first_len = FIRST
    second_len = length // first_len
    highs = length // 2 // first_len
    cos_one, sin_one = cos_sin(first_len, first_len, first_len)
    table_one = jnp.stack([cos_one, -sin_one])
    section_one = jnp.einsum("xca,mab->xmcb", table_one, blocks, precision=precision)
    cos_twist, sin_twist = cos_sin(first_len, second_len, length)
    real_one = section_one[0]
    imag_one = section_one[1]
    twisted = jnp.stack(
        [real_one * cos_twist + imag_one * sin_twist, imag_one * cos_twist - real_one * sin_twist]
    )
    cos_two, sin_two = cos_sin(highs, second_len, second_len)
    table_two = jnp.stack(
        [jnp.stack([cos_two, sin_two], axis=1), jnp.stack([-sin_two, cos_two], axis=1)]
    )
    return jnp.einsum("yqxb,xmcb->yqmc", table_two, twisted, precision=precision)


def correlate(own, gathered, prior, scale):
    _, groups_inp, groups_tm, count_s, inputs, lanes = own.shape
    rows = groups_inp * inputs
    cols = gathered.shape[1] * gathered.shape[4]
    depth = groups_tm * lanes
    out_groups = lanes // CH_AVG

    def kernel(*refs):
        own_ref, gat_ref = refs[0], refs[1]
        out_ref = refs[-1]
        group = pl.program_id(0)
        spectrum = pl.program_id(1)

        @pl.when(spectrum == 0)
        def _():
            if prior is None:
                out_ref[...] = jnp.zeros(out_ref.shape, out_ref.dtype)
            else:
                out_ref[...] = refs[2][...]

        def chunks(ref, part):
            pieces = [ref[part, :, t, 0].reshape(-1, lanes) for t in range(groups_tm)]
            return jnp.concatenate(pieces, axis=1)

        x0, x1 = chunks(own_ref, 0), chunks(own_ref, 1)
        c0, c1 = chunks(gat_ref, 0), chunks(gat_ref, 1)
        low = (lax.broadcasted_iota(jnp.int32, (1, depth), 1) % lanes) < CH_AVG

        def near(value, upper):
            return pltpu.roll(value, depth - CH_AVG if upper else CH_AVG, 1)

        def accumulate(upper):
            if upper:
                left_re = jnp.where(low, near(x0, True), x1)
                left_im = jnp.where(low, near(x1, True), -x0)
                right = jnp.where(low, near(c0, True), c1)
            else:
                left_re = jnp.where(low, x0, near(x1, False))
                left_im = jnp.where(low, x1, -near(x0, False))
                right = jnp.where(low, c0, near(c1, False))
            dims = (((1,), (1,)), ((), ()))
            real = lax.dot_general(left_re, right, dims, preferred_element_type=jnp.float32)
            imag = lax.dot_general(left_im, right, dims, preferred_element_type=jnp.float32)
            out_ref[0, 0] += real * scale
            out_ref[1, 0] += imag * scale

        for g in range(out_groups):
            pl.when(group == g)(lambda g=g: accumulate(g == 1))

    block_own = (2, groups_inp, groups_tm, 1, inputs, lanes)
    block_gat = (2, groups_inp, groups_tm, 1, gathered.shape[4], lanes)
    out_block = (2, 1, rows, cols)
    in_specs = [
        pl.BlockSpec(block_own, lambda g, s: (0, 0, 0, s, 0, 0)),
        pl.BlockSpec(block_gat, lambda g, s: (0, 0, 0, s, 0, 0)),
    ]
    operands = [own, gathered]
    aliases = {}
    if prior is not None:
        in_specs.append(pl.BlockSpec(out_block, lambda g, s: (0, g, 0, 0)))
        operands.append(prior)
        aliases = {2: 0}
    flops = 2 * 2 * rows * cols * depth * count_s * out_groups
    return pl.pallas_call(
        kernel,
        grid=(out_groups, count_s),
        in_specs=in_specs,
        out_specs=pl.BlockSpec(out_block, lambda g, s: (0, g, 0, 0)),
        out_shape=jax.ShapeDtypeStruct((2, out_groups, rows, cols), jnp.float32),
        input_output_aliases=aliases,
        compiler_params=pltpu.CompilerParams(vmem_limit_bytes=60 * 1024 * 1024),
        cost_estimate=pl.CostEstimate(
            flops=flops, transcendentals=0, bytes_accessed=2 * (own.size + gathered.size) * out_groups + 8 * rows * cols * out_groups
        ),
    )(*operands)


def shards(voltages, taps, flags):
    inputs = voltages.shape[0]
    tap_count = taps.shape[0]
    length = taps.shape[1]
    second_len = length // FIRST
    spectra_dev = voltages.shape[1] // length
    reach = tap_count - 1
    local = spectra_dev - reach
    precision = lax.Precision.HIGH
    blocked = voltages.reshape(inputs, spectra_dev, FIRST, second_len)
    leading = blocked[:, :reach].astype(jnp.bfloat16)
    following = passed_along(leading, "tm", -1)
    samples = blocked.astype(jnp.float32)
    tap_blocks = taps.reshape(tap_count, FIRST, second_len)

    def filtered(pieces, count):
        rows = []
        for spectrum in range(count):
            total = jnp.zeros((inputs, FIRST, second_len), jnp.float32)
            for offset in range(tap_count):
                total = total + tap_blocks[offset][None] * pieces[spectrum + offset]
            rows.append(total)
        return jnp.concatenate(rows, axis=0)

    scale = flags.astype(jnp.float32) / (8.0 * math.sqrt(length))
    groups_inp = lax.axis_size("inp")
    groups_tm = lax.axis_size("tm")
    count = float(groups_tm * spectra_dev * CH_AVG)

    def corner_turn(parts, count_s):
        spectra = (parts * jnp.tile(scale, count_s)[None, None, :, None]).astype(jnp.bfloat16)
        turned = lax.all_to_all(spectra, ("inp", "tm"), split_axis=1, concat_axis=1, tiled=True)
        own = turned.reshape(2, groups_inp, groups_tm, count_s, inputs, FIRST)
        return own, lax.all_gather(own, "bl", axis=4, tiled=True)

    own_pieces = [samples[:, j] for j in range(spectra_dev)]
    next_pieces = [following[:, j].astype(jnp.float32) for j in range(reach)]
    first_part = transform(filtered(own_pieces, local), length, precision)
    own, gathered = corner_turn(first_part, local)
    visibilities = correlate(own, gathered, None, 1.0 / count)
    second_part = transform(filtered(own_pieces[local:] + next_pieces, reach), length, precision)
    own, gathered = corner_turn(second_part, reach)
    visibilities = correlate(own, gathered, visibilities, 1.0 / count)
    return visibilities.reshape(2, FIRST // CH_AVG, groups_inp, inputs, -1)


def solution(mesh):
    in_specs = (P(("inp", "bl"), "tm"), P(), P(("inp", "bl")))
    out_specs = P(None, ("inp", "tm"), None, "bl", None)
    return jax.shard_map(shards, mesh=mesh, in_specs=in_specs, out_specs=out_specs, check_vma=False)
```

```python
import math

import jax
import jax.numpy as jnp
from jax import lax
from jax.experimental import pallas as pl
from jax.experimental.pallas import tpu as pltpu
from jax.sharding import PartitionSpec as P

CH_AVG = 64
FIRST = 128


def passed_along(value, axis, steps):
    count = lax.axis_size(axis)
    initial, last = (max(0, -steps), min(count, count - steps))
    return lax.ppermute(value, axis, [(source, source + steps) for source in range(initial, last)])


def cos_sin(height, breadth, period):
    grid = lax.broadcasted_iota(jnp.int32, (height, breadth), 0) * lax.broadcasted_iota(
        jnp.int32, (height, breadth), 1
    )
    angle = (grid % period).astype(jnp.float32) * (2.0 * math.pi / period)
    return (jnp.cos(angle), jnp.sin(angle))


def transform(blocks, length, precision):
    first_len = FIRST
    second_len = length // first_len
    highs = length // 2 // first_len
    cos_one, sin_one = cos_sin(first_len, first_len, first_len)
    table_one = jnp.stack([cos_one, -sin_one])
    section_one = jnp.einsum("xca,mab->xmcb", table_one, blocks, precision=precision)
    cos_twist, sin_twist = cos_sin(first_len, second_len, length)
    real_one = section_one[0]
    imag_one = section_one[1]
    twisted = jnp.stack(
        [real_one * cos_twist + imag_one * sin_twist, imag_one * cos_twist - real_one * sin_twist]
    )
    cos_two, sin_two = cos_sin(highs, second_len, second_len)
    table_two = jnp.stack(
        [jnp.stack([cos_two, sin_two], axis=1), jnp.stack([-sin_two, cos_two], axis=1)]
    )
    return jnp.einsum("yqxb,xmcb->yqmc", table_two, twisted, precision=precision)


def correlate(own, gathered, prior, scale):
    _, groups_inp, groups_tm, count_s, inputs, lanes = own.shape
    rows = groups_inp * inputs
    cols = gathered.shape[1] * gathered.shape[4]
    depth = groups_tm * lanes
    out_groups = lanes // CH_AVG

    def kernel(*refs):
        own_ref, gat_ref = refs[0], refs[1]
        out_ref = refs[-1]
        group = pl.program_id(0)
        spectrum = pl.program_id(1)

        @pl.when(spectrum == 0)
        def _():
            if prior is None:
                out_ref[...] = jnp.zeros(out_ref.shape, out_ref.dtype)
            else:
                out_ref[...] = refs[2][...]

        def chunks(ref, part):
            pieces = [ref[part, :, t, 0].reshape(-1, lanes) for t in range(groups_tm)]
            return jnp.concatenate(pieces, axis=1)

        x0, x1 = chunks(own_ref, 0), chunks(own_ref, 1)
        c0, c1 = chunks(gat_ref, 0), chunks(gat_ref, 1)
        low = (lax.broadcasted_iota(jnp.int32, (1, depth), 1) % lanes) < CH_AVG

        def near(value, upper):
            return pltpu.roll(value, depth - CH_AVG if upper else CH_AVG, 1)

        def accumulate(upper):
            if upper:
                left_re = jnp.where(low, near(x0, True), x1)
                left_im = jnp.where(low, near(x1, True), -x0)
                right = jnp.where(low, near(c0, True), c1)
            else:
                left_re = jnp.where(low, x0, near(x1, False))
                left_im = jnp.where(low, x1, -near(x0, False))
                right = jnp.where(low, c0, near(c1, False))
            dims = (((1,), (1,)), ((), ()))
            real = lax.dot_general(left_re, right, dims, preferred_element_type=jnp.float32)
            imag = lax.dot_general(left_im, right, dims, preferred_element_type=jnp.float32)
            out_ref[0, 0] += real * scale
            out_ref[1, 0] += imag * scale

        for g in range(out_groups):
            pl.when(group == g)(lambda g=g: accumulate(g == 1))

    block_own = (2, groups_inp, groups_tm, 1, inputs, lanes)
    block_gat = (2, groups_inp, groups_tm, 1, gathered.shape[4], lanes)
    out_block = (2, 1, rows, cols)
    in_specs = [
        pl.BlockSpec(block_own, lambda g, s: (0, 0, 0, s, 0, 0)),
        pl.BlockSpec(block_gat, lambda g, s: (0, 0, 0, s, 0, 0)),
    ]
    operands = [own, gathered]
    aliases = {}
    if prior is not None:
        in_specs.append(pl.BlockSpec(out_block, lambda g, s: (0, g, 0, 0)))
        operands.append(prior)
        aliases = {2: 0}
    flops = 2 * 2 * rows * cols * depth * count_s * out_groups
    return pl.pallas_call(
        kernel,
        grid=(out_groups, count_s),
        in_specs=in_specs,
        out_specs=pl.BlockSpec(out_block, lambda g, s: (0, g, 0, 0)),
        out_shape=jax.ShapeDtypeStruct((2, out_groups, rows, cols), jnp.float32),
        input_output_aliases=aliases,
        compiler_params=pltpu.CompilerParams(vmem_limit_bytes=60 * 1024 * 1024),
        cost_estimate=pl.CostEstimate(
            flops=flops, transcendentals=0, bytes_accessed=2 * (own.size + gathered.size) * out_groups + 8 * rows * cols * out_groups
        ),
    )(*operands)


def shards(voltages, taps, flags):
    inputs = voltages.shape[0]
    tap_count = taps.shape[0]
    length = taps.shape[1]
    second_len = length // FIRST
    spectra_dev = voltages.shape[1] // length
    reach = tap_count - 1
    local = spectra_dev - reach
    precision = lax.Precision.HIGH
    blocked = voltages.reshape(inputs, spectra_dev, FIRST, second_len)
    leading = voltages[:, : reach * length].astype(jnp.bfloat16)
    following = passed_along(leading, "tm", -1).reshape(inputs, reach, FIRST, second_len)
    samples = blocked.astype(jnp.float32)
    tap_blocks = taps.reshape(tap_count, FIRST, second_len)

    def filtered(pieces, count):
        rows = []
        for spectrum in range(count):
            total = jnp.zeros((inputs, FIRST, second_len), jnp.float32)
            for offset in range(tap_count):
                total = total + tap_blocks[offset][None] * pieces[spectrum + offset]
            rows.append(total)
        return jnp.concatenate(rows, axis=0)

    scale = flags.astype(jnp.float32) / (8.0 * math.sqrt(length))
    groups_inp = lax.axis_size("inp")
    groups_tm = lax.axis_size("tm")
    count = float(groups_tm * spectra_dev * CH_AVG)

    def corner_turn(parts, count_s):
        spectra = (parts * jnp.tile(scale, count_s)[None, None, :, None]).astype(jnp.bfloat16)
        turned = lax.all_to_all(spectra, ("inp", "tm"), split_axis=1, concat_axis=1, tiled=True)
        own = turned.reshape(2, groups_inp, groups_tm, count_s, inputs, FIRST)
        return own, lax.all_gather(own, "bl", axis=4, tiled=True)

    own_pieces = [samples[:, j] for j in range(spectra_dev)]
    next_pieces = [following[:, j].astype(jnp.float32) for j in range(reach)]
    first_part = transform(filtered(own_pieces, local), length, precision)
    own, gathered = corner_turn(first_part, local)
    visibilities = correlate(own, gathered, None, 1.0 / count)
    second_part = transform(filtered(own_pieces[local:] + next_pieces, reach), length, precision)
    own, gathered = corner_turn(second_part, reach)
    visibilities = correlate(own, gathered, visibilities, 1.0 / count)
    return visibilities.reshape(2, FIRST // CH_AVG, groups_inp, inputs, -1)


def solution(mesh):
    in_specs = (P(("inp", "bl"), "tm"), P(), P(("inp", "bl")))
    out_specs = P(None, ("inp", "tm"), None, "bl", None)
    return jax.shard_map(shards, mesh=mesh, in_specs=in_specs, out_specs=out_specs, check_vma=False)
```

```python
import math

import jax
import jax.numpy as jnp
from jax import lax
from jax.experimental import pallas as pl
from jax.experimental.pallas import tpu as pltpu
from jax.sharding import PartitionSpec as P

CH_AVG = 64
FIRST = 128


def passed_along(value, axis, steps):
    count = lax.axis_size(axis)
    initial, last = (max(0, -steps), min(count, count - steps))
    return lax.ppermute(value, axis, [(source, source + steps) for source in range(initial, last)])


def cos_sin(height, breadth, period):
    grid = lax.broadcasted_iota(jnp.int32, (height, breadth), 0) * lax.broadcasted_iota(
        jnp.int32, (height, breadth), 1
    )
    angle = (grid % period).astype(jnp.float32) * (2.0 * math.pi / period)
    return (jnp.cos(angle), jnp.sin(angle))


def transform(blocks, length, precision):
    first_len = FIRST
    second_len = length // first_len
    highs = length // 2 // first_len
    cos_one, sin_one = cos_sin(first_len, first_len, first_len)
    table_one = jnp.stack([cos_one, -sin_one])
    section_one = jnp.einsum("xca,mab->xmcb", table_one, blocks, precision=precision)
    cos_twist, sin_twist = cos_sin(first_len, second_len, length)
    real_one = section_one[0]
    imag_one = section_one[1]
    twisted = jnp.stack(
        [real_one * cos_twist + imag_one * sin_twist, imag_one * cos_twist - real_one * sin_twist]
    )
    cos_two, sin_two = cos_sin(highs, second_len, second_len)
    table_two = jnp.stack(
        [jnp.stack([cos_two, sin_two], axis=1), jnp.stack([-sin_two, cos_two], axis=1)]
    )
    return jnp.einsum("yqxb,xmcb->yqmc", table_two, twisted, precision=precision)


def correlate(own, gathered, prior, scale):
    _, groups_inp, groups_tm, count_s, inputs, lanes = own.shape
    rows = groups_inp * inputs
    cols = gathered.shape[1] * gathered.shape[4]
    depth = groups_tm * lanes
    out_groups = lanes // CH_AVG

    def kernel(*refs):
        own_ref, gat_ref = refs[0], refs[1]
        out_ref = refs[-1]
        group = pl.program_id(0)
        spectrum = pl.program_id(1)

        @pl.when(spectrum == 0)
        def _():
            if prior is None:
                out_ref[...] = jnp.zeros(out_ref.shape, out_ref.dtype)
            else:
                out_ref[...] = refs[2][...]

        def chunks(ref, part):
            pieces = [ref[part, :, t, 0].reshape(-1, lanes) for t in range(groups_tm)]
            return jnp.concatenate(pieces, axis=1)

        x0, x1 = chunks(own_ref, 0), chunks(own_ref, 1)
        c0, c1 = chunks(gat_ref, 0), chunks(gat_ref, 1)
        low = (lax.broadcasted_iota(jnp.int32, (1, depth), 1) % lanes) < CH_AVG

        def near(value, upper):
            return pltpu.roll(value, depth - CH_AVG if upper else CH_AVG, 1)

        def accumulate(upper):
            if upper:
                left_re = jnp.where(low, near(x0, True), x1)
                left_im = jnp.where(low, near(x1, True), -x0)
                right = jnp.where(low, near(c0, True), c1)
            else:
                left_re = jnp.where(low, x0, near(x1, False))
                left_im = jnp.where(low, x1, -near(x0, False))
                right = jnp.where(low, c0, near(c1, False))
            dims = (((1,), (1,)), ((), ()))
            real = lax.dot_general(left_re, right, dims, preferred_element_type=jnp.float32)
            imag = lax.dot_general(left_im, right, dims, preferred_element_type=jnp.float32)
            out_ref[0, 0] += real * scale
            out_ref[1, 0] += imag * scale

        for g in range(out_groups):
            pl.when(group == g)(lambda g=g: accumulate(g == 1))

    block_own = (2, groups_inp, groups_tm, 1, inputs, lanes)
    block_gat = (2, groups_inp, groups_tm, 1, gathered.shape[4], lanes)
    out_block = (2, 1, rows, cols)
    in_specs = [
        pl.BlockSpec(block_own, lambda g, s: (0, 0, 0, s, 0, 0)),
        pl.BlockSpec(block_gat, lambda g, s: (0, 0, 0, s, 0, 0)),
    ]
    operands = [own, gathered]
    aliases = {}
    if prior is not None:
        in_specs.append(pl.BlockSpec(out_block, lambda g, s: (0, g, 0, 0)))
        operands.append(prior)
        aliases = {2: 0}
    flops = 2 * 2 * rows * cols * depth * count_s * out_groups
    return pl.pallas_call(
        kernel,
        grid=(out_groups, count_s),
        in_specs=in_specs,
        out_specs=pl.BlockSpec(out_block, lambda g, s: (0, g, 0, 0)),
        out_shape=jax.ShapeDtypeStruct((2, out_groups, rows, cols), jnp.float32),
        input_output_aliases=aliases,
        compiler_params=pltpu.CompilerParams(vmem_limit_bytes=60 * 1024 * 1024),
        cost_estimate=pl.CostEstimate(
            flops=flops, transcendentals=0, bytes_accessed=2 * (own.size + gathered.size) * out_groups + 8 * rows * cols * out_groups
        ),
    )(*operands)


def shards(voltages, taps, flags):
    inputs = voltages.shape[0]
    tap_count = taps.shape[0]
    length = taps.shape[1]
    second_len = length // FIRST
    spectra_dev = voltages.shape[1] // length
    reach = tap_count - 1
    local = spectra_dev - reach
    precision = lax.Precision.HIGH
    blocked = voltages.reshape(inputs, spectra_dev, FIRST, second_len)
    assert spectra_dev >= tap_count and reach >= 2
    ahead = reach - 1
    leading = voltages[:, : ahead * length].astype(jnp.bfloat16)
    following = passed_along(leading, "tm", -1).reshape(inputs, ahead, FIRST, second_len)
    blocks_tm = lax.axis_size("tm")
    trailing = voltages[:, (spectra_dev - 1) * length :].astype(jnp.bfloat16)
    previous = lax.ppermute(
        trailing, "tm", [(source, (source + 1) % blocks_tm) for source in range(blocks_tm)]
    ).reshape(inputs, FIRST, second_len)
    samples = blocked.astype(jnp.float32)
    tap_blocks = taps.reshape(tap_count, FIRST, second_len)

    def filtered(pieces, count):
        rows = []
        for spectrum in range(count):
            total = jnp.zeros((inputs, FIRST, second_len), jnp.float32)
            for offset in range(tap_count):
                total = total + tap_blocks[offset][None] * pieces[spectrum + offset]
            rows.append(total)
        return jnp.concatenate(rows, axis=0)

    scale = flags.astype(jnp.float32) / (8.0 * math.sqrt(length))
    groups_inp = lax.axis_size("inp")
    groups_tm = lax.axis_size("tm")
    count = float(groups_tm * spectra_dev * CH_AVG)

    def corner_turn(parts, count_s):
        spectra = (parts * jnp.tile(scale, count_s)[None, None, :, None]).astype(jnp.bfloat16)
        turned = lax.all_to_all(spectra, ("inp", "tm"), split_axis=1, concat_axis=1, tiled=True)
        own = turned.reshape(2, groups_inp, groups_tm, count_s, inputs, FIRST)
        return own, lax.all_gather(own, "bl", axis=4, tiled=True)

    own_pieces = [samples[:, j] for j in range(spectra_dev)]
    keep = (lax.axis_index("tm") != 0).astype(jnp.float32)
    wrapped = [previous.astype(jnp.float32)] + [piece * keep for piece in own_pieces[:reach]]
    first_part = transform(
        jnp.concatenate([filtered(own_pieces, 1), filtered(wrapped, 1)], axis=0), length, precision
    )
    own, gathered = corner_turn(first_part, 2)
    visibilities = correlate(own, gathered, None, 1.0 / count)
    next_pieces = [following[:, j].astype(jnp.float32) for j in range(ahead)]
    later = spectra_dev - 2
    second_part = transform(filtered(own_pieces[1:] + next_pieces, later), length, precision)
    own, gathered = corner_turn(second_part, later)
    visibilities = correlate(own, gathered, visibilities, 1.0 / count)
    return visibilities.reshape(2, FIRST // CH_AVG, groups_inp, inputs, -1)


def solution(mesh):
    in_specs = (P(("inp", "bl"), "tm"), P(), P(("inp", "bl")))
    out_specs = P(None, ("inp", "tm"), None, "bl", None)
    return jax.shard_map(shards, mesh=mesh, in_specs=in_specs, out_specs=out_specs, check_vma=False)
```

```python
import math

import jax
import jax.numpy as jnp
from jax import lax
from jax.experimental import pallas as pl
from jax.experimental.pallas import tpu as pltpu
from jax.sharding import PartitionSpec as P

CH_AVG = 64
FIRST = 128


def passed_along(value, axis, steps):
    count = lax.axis_size(axis)
    initial, last = (max(0, -steps), min(count, count - steps))
    return lax.ppermute(value, axis, [(source, source + steps) for source in range(initial, last)])


def cos_sin(height, breadth, period):
    grid = lax.broadcasted_iota(jnp.int32, (height, breadth), 0) * lax.broadcasted_iota(
        jnp.int32, (height, breadth), 1
    )
    angle = (grid % period).astype(jnp.float32) * (2.0 * math.pi / period)
    return (jnp.cos(angle), jnp.sin(angle))


def transform(blocks, length, precision):
    first_len = FIRST
    second_len = length // first_len
    highs = length // 2 // first_len
    cos_one, sin_one = cos_sin(first_len, first_len, first_len)
    table_one = jnp.stack([cos_one, -sin_one])
    section_one = jnp.einsum("xca,mab->xmcb", table_one, blocks, precision=precision)
    cos_twist, sin_twist = cos_sin(first_len, second_len, length)
    real_one = section_one[0]
    imag_one = section_one[1]
    twisted = jnp.stack(
        [real_one * cos_twist + imag_one * sin_twist, imag_one * cos_twist - real_one * sin_twist]
    )
    cos_two, sin_two = cos_sin(highs, second_len, second_len)
    table_two = jnp.stack(
        [jnp.stack([cos_two, sin_two], axis=1), jnp.stack([-sin_two, cos_two], axis=1)]
    )
    return jnp.einsum("yqxb,xmcb->yqmc", table_two, twisted, precision=precision)


def correlate(own, gathered, prior, scale):
    _, groups_inp, groups_tm, count_s, inputs, lanes = own.shape
    rows = groups_inp * inputs
    cols = gathered.shape[1] * gathered.shape[4]
    depth = groups_tm * lanes
    out_groups = lanes // CH_AVG

    def kernel(*refs):
        own_ref, gat_ref = refs[0], refs[1]
        out_ref = refs[-1]
        group = pl.program_id(0)
        spectrum = pl.program_id(1)

        @pl.when(spectrum == 0)
        def _():
            if prior is None:
                out_ref[...] = jnp.zeros(out_ref.shape, out_ref.dtype)
            else:
                out_ref[...] = refs[2][...]

        def chunks(ref, part):
            pieces = [ref[part, :, t, 0].reshape(-1, lanes) for t in range(groups_tm)]
            return jnp.concatenate(pieces, axis=1)

        x0, x1 = chunks(own_ref, 0), chunks(own_ref, 1)
        c0, c1 = chunks(gat_ref, 0), chunks(gat_ref, 1)
        low = (lax.broadcasted_iota(jnp.int32, (1, depth), 1) % lanes) < CH_AVG

        def near(value, upper):
            return pltpu.roll(value, depth - CH_AVG if upper else CH_AVG, 1)

        def accumulate(upper):
            if upper:
                left_re = jnp.where(low, near(x0, True), x1)
                left_im = jnp.where(low, near(x1, True), -x0)
                right = jnp.where(low, near(c0, True), c1)
            else:
                left_re = jnp.where(low, x0, near(x1, False))
                left_im = jnp.where(low, x1, -near(x0, False))
                right = jnp.where(low, c0, near(c1, False))
            dims = (((1,), (1,)), ((), ()))
            real = lax.dot_general(left_re, right, dims, preferred_element_type=jnp.float32)
            imag = lax.dot_general(left_im, right, dims, preferred_element_type=jnp.float32)
            out_ref[0, 0] += real * scale
            out_ref[1, 0] += imag * scale

        for g in range(out_groups):
            pl.when(group == g)(lambda g=g: accumulate(g == 1))

    block_own = (2, groups_inp, groups_tm, 1, inputs, lanes)
    block_gat = (2, groups_inp, groups_tm, 1, gathered.shape[4], lanes)
    out_block = (2, 1, rows, cols)
    in_specs = [
        pl.BlockSpec(block_own, lambda g, s: (0, 0, 0, s, 0, 0)),
        pl.BlockSpec(block_gat, lambda g, s: (0, 0, 0, s, 0, 0)),
    ]
    operands = [own, gathered]
    aliases = {}
    if prior is not None:
        in_specs.append(pl.BlockSpec(out_block, lambda g, s: (0, g, 0, 0)))
        operands.append(prior)
        aliases = {2: 0}
    flops = 2 * 2 * rows * cols * depth * count_s * out_groups
    return pl.pallas_call(
        kernel,
        grid=(out_groups, count_s),
        in_specs=in_specs,
        out_specs=pl.BlockSpec(out_block, lambda g, s: (0, g, 0, 0)),
        out_shape=jax.ShapeDtypeStruct((2, out_groups, rows, cols), jnp.float32),
        input_output_aliases=aliases,
        compiler_params=pltpu.CompilerParams(vmem_limit_bytes=60 * 1024 * 1024),
        cost_estimate=pl.CostEstimate(
            flops=flops, transcendentals=0, bytes_accessed=2 * (own.size + gathered.size) * out_groups + 8 * rows * cols * out_groups
        ),
    )(*operands)


def shards(voltages, taps, flags):
    inputs = voltages.shape[0]
    tap_count = taps.shape[0]
    length = taps.shape[1]
    second_len = length // FIRST
    spectra_dev = voltages.shape[1] // length
    reach = tap_count - 1
    local = spectra_dev - reach
    precision = lax.Precision.HIGH
    blocked = voltages.reshape(inputs, spectra_dev, FIRST, second_len)
    assert spectra_dev >= tap_count and reach >= 2
    ahead = reach - 1
    leading = voltages[:, : ahead * length].astype(jnp.bfloat16)
    following = passed_along(leading, "tm", -1).reshape(inputs, ahead, FIRST, second_len)
    blocks_tm = lax.axis_size("tm")
    trailing = voltages[:, (spectra_dev - 1) * length :].astype(jnp.bfloat16)
    previous = lax.ppermute(
        trailing, "tm", [(source, (source + 1) % blocks_tm) for source in range(blocks_tm)]
    ).reshape(inputs, FIRST, second_len)
    samples = blocked.astype(jnp.float32)
    tap_blocks = taps.reshape(tap_count, FIRST, second_len)

    def filtered(pieces, count):
        rows = []
        for spectrum in range(count):
            total = jnp.zeros((inputs, FIRST, second_len), jnp.float32)
            for offset in range(tap_count):
                total = total + tap_blocks[offset][None] * pieces[spectrum + offset]
            rows.append(total)
        return jnp.concatenate(rows, axis=0)

    scale = flags.astype(jnp.float32) / (8.0 * math.sqrt(length))
    groups_inp = lax.axis_size("inp")
    groups_tm = lax.axis_size("tm")
    count = float(groups_tm * spectra_dev * CH_AVG)

    def corner_turn(parts, count_s):
        spectra = (parts * jnp.tile(scale, count_s)[None, None, :, None]).astype(jnp.bfloat16)
        turned = lax.all_to_all(spectra, ("inp", "tm"), split_axis=1, concat_axis=1, tiled=True)
        own = turned.reshape(2, groups_inp, groups_tm, count_s, inputs, FIRST)
        return own, lax.all_gather(own, "bl", axis=4, tiled=True)

    own_pieces = [samples[:, j] for j in range(spectra_dev)]
    keep = (lax.axis_index("tm") != 0).astype(jnp.float32)
    wrapped = [previous.astype(jnp.float32)] + [piece * keep for piece in own_pieces[:reach]]
    first_part = transform(filtered(own_pieces, 1), length, precision)
    own, gathered = corner_turn(first_part, 1)
    visibilities = correlate(own, gathered, None, 1.0 / count)
    next_pieces = [following[:, j].astype(jnp.float32) for j in range(ahead)]
    later = spectra_dev - 2
    second_part = transform(
        jnp.concatenate([filtered(wrapped, 1), filtered(own_pieces[1:] + next_pieces, later)], axis=0),
        length,
        precision,
    )
    own, gathered = corner_turn(second_part, later + 1)
    visibilities = correlate(own, gathered, visibilities, 1.0 / count)
    return visibilities.reshape(2, FIRST // CH_AVG, groups_inp, inputs, -1)


def solution(mesh):
    in_specs = (P(("inp", "bl"), "tm"), P(), P(("inp", "bl")))
    out_specs = P(None, ("inp", "tm"), None, "bl", None)
    return jax.shard_map(shards, mesh=mesh, in_specs=in_specs, out_specs=out_specs, check_vma=False)
```

```python
import math

import jax
import jax.numpy as jnp
from jax import lax
from jax.experimental import pallas as pl
from jax.experimental.pallas import tpu as pltpu
from jax.sharding import PartitionSpec as P

CH_AVG = 64
FIRST = 128


def passed_along(value, axis, steps):
    count = lax.axis_size(axis)
    initial, last = (max(0, -steps), min(count, count - steps))
    return lax.ppermute(value, axis, [(source, source + steps) for source in range(initial, last)])


def cos_sin(height, breadth, period):
    grid = lax.broadcasted_iota(jnp.int32, (height, breadth), 0) * lax.broadcasted_iota(
        jnp.int32, (height, breadth), 1
    )
    angle = (grid % period).astype(jnp.float32) * (2.0 * math.pi / period)
    return (jnp.cos(angle), jnp.sin(angle))


def transform(blocks, length, precision):
    first_len = FIRST
    second_len = length // first_len
    highs = length // 2 // first_len
    cos_one, sin_one = cos_sin(first_len, first_len, first_len)
    table_one = jnp.stack([cos_one, -sin_one])
    section_one = jnp.einsum("xca,mab->xmcb", table_one, blocks, precision=precision)
    cos_twist, sin_twist = cos_sin(first_len, second_len, length)
    real_one = section_one[0]
    imag_one = section_one[1]
    twisted = jnp.stack(
        [real_one * cos_twist + imag_one * sin_twist, imag_one * cos_twist - real_one * sin_twist]
    )
    cos_two, sin_two = cos_sin(highs, second_len, second_len)
    table_two = jnp.stack(
        [jnp.stack([cos_two, sin_two], axis=1), jnp.stack([-sin_two, cos_two], axis=1)]
    )
    return jnp.einsum("yqxb,xmcb->yqmc", table_two, twisted, precision=precision)


def correlate(own, gathered, prior, scale):
    _, groups_inp, groups_tm, count_s, inputs, lanes = own.shape
    rows = groups_inp * inputs
    cols = gathered.shape[1] * gathered.shape[4]
    depth = groups_tm * lanes
    out_groups = lanes // CH_AVG

    def kernel(*refs):
        own_ref, gat_ref = refs[0], refs[1]
        out_ref = refs[-1]
        group = pl.program_id(0)
        spectrum = pl.program_id(1)

        @pl.when(spectrum == 0)
        def _():
            if prior is None:
                out_ref[...] = jnp.zeros(out_ref.shape, out_ref.dtype)
            else:
                out_ref[...] = refs[2][...]

        def chunks(ref, part):
            pieces = [ref[part, :, t, 0].reshape(-1, lanes) for t in range(groups_tm)]
            return jnp.concatenate(pieces, axis=1)

        x0, x1 = chunks(own_ref, 0), chunks(own_ref, 1)
        c0, c1 = chunks(gat_ref, 0), chunks(gat_ref, 1)
        low = (lax.broadcasted_iota(jnp.int32, (1, depth), 1) % lanes) < CH_AVG

        def near(value, upper):
            return pltpu.roll(value, depth - CH_AVG if upper else CH_AVG, 1)

        def accumulate(upper):
            if upper:
                left_re = jnp.where(low, near(x0, True), x1)
                left_im = jnp.where(low, near(x1, True), -x0)
                right = jnp.where(low, near(c0, True), c1)
            else:
                left_re = jnp.where(low, x0, near(x1, False))
                left_im = jnp.where(low, x1, -near(x0, False))
                right = jnp.where(low, c0, near(c1, False))
            dims = (((1,), (1,)), ((), ()))
            real = lax.dot_general(left_re, right, dims, preferred_element_type=jnp.float32)
            imag = lax.dot_general(left_im, right, dims, preferred_element_type=jnp.float32)
            out_ref[0, 0] += real * scale
            out_ref[1, 0] += imag * scale

        for g in range(out_groups):
            pl.when(group == g)(lambda g=g: accumulate(g == 1))

    block_own = (2, groups_inp, groups_tm, 1, inputs, lanes)
    block_gat = (2, groups_inp, groups_tm, 1, gathered.shape[4], lanes)
    out_block = (2, 1, rows, cols)
    in_specs = [
        pl.BlockSpec(block_own, lambda g, s: (0, 0, 0, s, 0, 0)),
        pl.BlockSpec(block_gat, lambda g, s: (0, 0, 0, s, 0, 0)),
    ]
    operands = [own, gathered]
    aliases = {}
    if prior is not None:
        in_specs.append(pl.BlockSpec(out_block, lambda g, s: (0, g, 0, 0)))
        operands.append(prior)
        aliases = {2: 0}
    flops = 2 * 2 * rows * cols * depth * count_s * out_groups
    return pl.pallas_call(
        kernel,
        grid=(out_groups, count_s),
        in_specs=in_specs,
        out_specs=pl.BlockSpec(out_block, lambda g, s: (0, g, 0, 0)),
        out_shape=jax.ShapeDtypeStruct((2, out_groups, rows, cols), jnp.float32),
        input_output_aliases=aliases,
        compiler_params=pltpu.CompilerParams(vmem_limit_bytes=60 * 1024 * 1024),
        cost_estimate=pl.CostEstimate(
            flops=flops, transcendentals=0, bytes_accessed=2 * (own.size + gathered.size) * out_groups + 8 * rows * cols * out_groups
        ),
    )(*operands)


def shards(voltages, taps, flags):
    inputs = voltages.shape[0]
    tap_count = taps.shape[0]
    length = taps.shape[1]
    second_len = length // FIRST
    spectra_dev = voltages.shape[1] // length
    reach = tap_count - 1
    local = spectra_dev - reach
    precision = lax.Precision.HIGH
    blocked = voltages.reshape(inputs, spectra_dev, FIRST, second_len)
    assert spectra_dev >= tap_count and reach >= 2
    ahead = reach - 1
    leading = voltages[:, : ahead * length].astype(jnp.bfloat16)
    following = passed_along(leading, "tm", -1).reshape(inputs, ahead, FIRST, second_len)
    blocks_tm = lax.axis_size("tm")
    trailing = voltages[:, (spectra_dev - 1) * length :].astype(jnp.bfloat16)
    previous = lax.ppermute(
        trailing, "tm", [(source, (source + 1) % blocks_tm) for source in range(blocks_tm)]
    ).reshape(inputs, FIRST, second_len)
    samples = blocked.astype(jnp.float32)
    tap_blocks = taps.reshape(tap_count, FIRST, second_len)

    def filtered(pieces, count):
        rows = []
        for spectrum in range(count):
            total = jnp.zeros((inputs, FIRST, second_len), jnp.float32)
            for offset in range(tap_count):
                total = total + tap_blocks[offset][None] * pieces[spectrum + offset]
            rows.append(total)
        return jnp.concatenate(rows, axis=0)

    scale = flags.astype(jnp.float32) / (8.0 * math.sqrt(length))
    groups_inp = lax.axis_size("inp")
    groups_tm = lax.axis_size("tm")
    count = float(groups_tm * spectra_dev * CH_AVG)

    def corner_turn(parts, count_s):
        spectra = (parts * jnp.tile(scale, count_s)[None, None, :, None]).astype(jnp.bfloat16)
        turned = lax.all_to_all(spectra, ("inp", "tm"), split_axis=1, concat_axis=1, tiled=True)
        own = turned.reshape(2, groups_inp, groups_tm, count_s, inputs, FIRST)
        return own, lax.all_gather(own, "bl", axis=4, tiled=True)

    own_pieces = [samples[:, j] for j in range(spectra_dev)]
    keep = (lax.axis_index("tm") != 0).astype(jnp.float32)
    wrapped = [previous.astype(jnp.float32)] + [piece * keep for piece in own_pieces[:reach]]
    first_part = transform(filtered(own_pieces, 1), length, precision)
    own, gathered = corner_turn(first_part, 1)
    visibilities = correlate(own, gathered, None, 1.0 / count)
    next_pieces = [following[:, j].astype(jnp.float32) for j in range(ahead)]
    later = spectra_dev - 2
    rest = own_pieces[1:] + next_pieces
    second_part = jnp.concatenate(
        [transform(filtered(wrapped, 1), length, precision)]
        + [transform(filtered(rest[j:], 1), length, precision) for j in range(later)],
        axis=2,
    )
    own, gathered = corner_turn(second_part, later + 1)
    visibilities = correlate(own, gathered, visibilities, 1.0 / count)
    return visibilities.reshape(2, FIRST // CH_AVG, groups_inp, inputs, -1)


def solution(mesh):
    in_specs = (P(("inp", "bl"), "tm"), P(), P(("inp", "bl")))
    out_specs = P(None, ("inp", "tm"), None, "bl", None)
    return jax.shard_map(shards, mesh=mesh, in_specs=in_specs, out_specs=out_specs, check_vma=False)
```

```python
import math

import jax
import jax.numpy as jnp
from jax import lax
from jax.experimental import pallas as pl
from jax.experimental.pallas import tpu as pltpu
from jax.sharding import PartitionSpec as P

CH_AVG = 64
FIRST = 128


def passed_along(value, axis, steps):
    count = lax.axis_size(axis)
    initial, last = (max(0, -steps), min(count, count - steps))
    return lax.ppermute(value, axis, [(source, source + steps) for source in range(initial, last)])


def cos_sin(height, breadth, period):
    grid = lax.broadcasted_iota(jnp.int32, (height, breadth), 0) * lax.broadcasted_iota(
        jnp.int32, (height, breadth), 1
    )
    angle = (grid % period).astype(jnp.float32) * (2.0 * math.pi / period)
    return (jnp.cos(angle), jnp.sin(angle))


def transform(blocks, length, precision):
    first_len = FIRST
    second_len = length // first_len
    highs = length // 2 // first_len
    cos_one, sin_one = cos_sin(first_len, first_len, first_len)
    table_one = jnp.stack([cos_one, -sin_one])
    section_one = jnp.einsum("xca,mab->xmcb", table_one, blocks, precision=precision)
    cos_twist, sin_twist = cos_sin(first_len, second_len, length)
    real_one = section_one[0]
    imag_one = section_one[1]
    twisted = jnp.stack(
        [real_one * cos_twist + imag_one * sin_twist, imag_one * cos_twist - real_one * sin_twist]
    )
    cos_two, sin_two = cos_sin(highs, second_len, second_len)
    table_two = jnp.stack(
        [jnp.stack([cos_two, sin_two], axis=1), jnp.stack([-sin_two, cos_two], axis=1)]
    )
    return jnp.einsum("yqxb,xmcb->yqmc", table_two, twisted, precision=precision)


def correlate(own, gathered, prior, scale):
    _, groups_inp, groups_tm, count_s, inputs, lanes = own.shape
    rows = groups_inp * inputs
    cols = gathered.shape[1] * gathered.shape[4]
    depth = groups_tm * lanes
    out_groups = lanes // CH_AVG

    def kernel(*refs):
        own_ref, gat_ref = refs[0], refs[1]
        out_ref = refs[-1]
        group = pl.program_id(0)
        spectrum = pl.program_id(1)

        @pl.when(spectrum == 0)
        def _():
            if prior is None:
                out_ref[...] = jnp.zeros(out_ref.shape, out_ref.dtype)
            else:
                out_ref[...] = refs[2][...]

        def chunks(ref, part):
            pieces = [ref[part, :, t, 0].reshape(-1, lanes) for t in range(groups_tm)]
            return jnp.concatenate(pieces, axis=1)

        x0, x1 = chunks(own_ref, 0), chunks(own_ref, 1)
        c0, c1 = chunks(gat_ref, 0), chunks(gat_ref, 1)
        low = (lax.broadcasted_iota(jnp.int32, (1, depth), 1) % lanes) < CH_AVG

        def near(value, upper):
            return pltpu.roll(value, depth - CH_AVG if upper else CH_AVG, 1)

        def accumulate(upper):
            if upper:
                left_re = jnp.where(low, near(x0, True), x1)
                left_im = jnp.where(low, near(x1, True), -x0)
                right = jnp.where(low, near(c0, True), c1)
            else:
                left_re = jnp.where(low, x0, near(x1, False))
                left_im = jnp.where(low, x1, -near(x0, False))
                right = jnp.where(low, c0, near(c1, False))
            dims = (((1,), (1,)), ((), ()))
            real = lax.dot_general(left_re, right, dims, preferred_element_type=jnp.float32)
            imag = lax.dot_general(left_im, right, dims, preferred_element_type=jnp.float32)
            out_ref[0, 0] += real * scale
            out_ref[1, 0] += imag * scale

        for g in range(out_groups):
            pl.when(group == g)(lambda g=g: accumulate(g == 1))

    block_own = (2, groups_inp, groups_tm, 1, inputs, lanes)
    block_gat = (2, groups_inp, groups_tm, 1, gathered.shape[4], lanes)
    out_block = (2, 1, rows, cols)
    in_specs = [
        pl.BlockSpec(block_own, lambda g, s: (0, 0, 0, s, 0, 0)),
        pl.BlockSpec(block_gat, lambda g, s: (0, 0, 0, s, 0, 0)),
    ]
    operands = [own, gathered]
    aliases = {}
    if prior is not None:
        in_specs.append(pl.BlockSpec(out_block, lambda g, s: (0, g, 0, 0)))
        operands.append(prior)
        aliases = {2: 0}
    flops = 2 * 2 * rows * cols * depth * count_s * out_groups
    return pl.pallas_call(
        kernel,
        grid=(out_groups, count_s),
        in_specs=in_specs,
        out_specs=pl.BlockSpec(out_block, lambda g, s: (0, g, 0, 0)),
        out_shape=jax.ShapeDtypeStruct((2, out_groups, rows, cols), jnp.float32),
        input_output_aliases=aliases,
        compiler_params=pltpu.CompilerParams(vmem_limit_bytes=60 * 1024 * 1024),
        cost_estimate=pl.CostEstimate(
            flops=flops, transcendentals=0, bytes_accessed=2 * (own.size + gathered.size) * out_groups + 8 * rows * cols * out_groups
        ),
    )(*operands)


def shards(voltages, taps, flags):
    inputs = voltages.shape[0]
    tap_count = taps.shape[0]
    length = taps.shape[1]
    second_len = length // FIRST
    spectra_dev = voltages.shape[1] // length
    reach = tap_count - 1
    local = spectra_dev - reach
    precision = lax.Precision.HIGH
    blocked = voltages.reshape(inputs, spectra_dev, FIRST, second_len)
    assert spectra_dev >= tap_count and reach >= 2
    ahead = reach - 1
    leading = voltages[:, : ahead * length].astype(jnp.bfloat16)
    following = passed_along(leading, "tm", -1).reshape(inputs, ahead, FIRST, second_len)
    blocks_tm = lax.axis_size("tm")
    trailing = voltages[:, (spectra_dev - 1) * length :].astype(jnp.bfloat16)
    previous = lax.ppermute(
        trailing, "tm", [(source, (source + 1) % blocks_tm) for source in range(blocks_tm)]
    ).reshape(inputs, FIRST, second_len)
    samples = lax.optimization_barrier(blocked).astype(jnp.float32)
    tap_blocks = taps.reshape(tap_count, FIRST, second_len)

    def filtered(pieces, count):
        rows = []
        for spectrum in range(count):
            total = jnp.zeros((inputs, FIRST, second_len), jnp.float32)
            for offset in range(tap_count):
                total = total + tap_blocks[offset][None] * pieces[spectrum + offset]
            rows.append(total)
        return jnp.concatenate(rows, axis=0)

    scale = flags.astype(jnp.float32) / (8.0 * math.sqrt(length))
    groups_inp = lax.axis_size("inp")
    groups_tm = lax.axis_size("tm")
    count = float(groups_tm * spectra_dev * CH_AVG)

    def corner_turn(parts, count_s):
        spectra = (parts * jnp.tile(scale, count_s)[None, None, :, None]).astype(jnp.bfloat16)
        turned = lax.all_to_all(spectra, ("inp", "tm"), split_axis=1, concat_axis=1, tiled=True)
        own = turned.reshape(2, groups_inp, groups_tm, count_s, inputs, FIRST)
        return own, lax.all_gather(own, "bl", axis=4, tiled=True)

    own_pieces = [samples[:, j] for j in range(spectra_dev)]
    keep = (lax.axis_index("tm") != 0).astype(jnp.float32)
    wrapped = [previous.astype(jnp.float32)] + [piece * keep for piece in own_pieces[:reach]]
    first_part = transform(filtered(own_pieces, 1), length, precision)
    own, gathered = corner_turn(first_part, 1)
    visibilities = correlate(own, gathered, None, 1.0 / count)
    next_pieces = [following[:, j].astype(jnp.float32) for j in range(ahead)]
    later = spectra_dev - 2
    rest = own_pieces[1:] + next_pieces
    second_part = jnp.concatenate(
        [transform(filtered(wrapped, 1), length, precision)]
        + [transform(filtered(rest[j:], 1), length, precision) for j in range(later)],
        axis=2,
    )
    own, gathered = corner_turn(second_part, later + 1)
    visibilities = correlate(own, gathered, visibilities, 1.0 / count)
    return visibilities.reshape(2, FIRST // CH_AVG, groups_inp, inputs, -1)


def solution(mesh):
    in_specs = (P(("inp", "bl"), "tm"), P(), P(("inp", "bl")))
    out_specs = P(None, ("inp", "tm"), None, "bl", None)
    return jax.shard_map(shards, mesh=mesh, in_specs=in_specs, out_specs=out_specs, check_vma=False)
```

```python
import math

import jax
import jax.numpy as jnp
from jax import lax
from jax.experimental import pallas as pl
from jax.experimental.pallas import tpu as pltpu
from jax.sharding import PartitionSpec as P

CH_AVG = 64
FIRST = 128


def passed_along(value, axis, steps):
    count = lax.axis_size(axis)
    initial, last = (max(0, -steps), min(count, count - steps))
    return lax.ppermute(value, axis, [(source, source + steps) for source in range(initial, last)])


def cos_sin(height, breadth, period):
    grid = lax.broadcasted_iota(jnp.int32, (height, breadth), 0) * lax.broadcasted_iota(
        jnp.int32, (height, breadth), 1
    )
    angle = (grid % period).astype(jnp.float32) * (2.0 * math.pi / period)
    return (jnp.cos(angle), jnp.sin(angle))


def transform(blocks, length, precision):
    first_len = FIRST
    second_len = length // first_len
    highs = length // 2 // first_len
    cos_one, sin_one = cos_sin(first_len, first_len, first_len)
    table_one = jnp.stack([cos_one, -sin_one])
    section_one = jnp.einsum("xca,mab->xmcb", table_one, blocks, precision=precision)
    cos_twist, sin_twist = cos_sin(first_len, second_len, length)
    real_one = section_one[0]
    imag_one = section_one[1]
    twisted = jnp.stack(
        [real_one * cos_twist + imag_one * sin_twist, imag_one * cos_twist - real_one * sin_twist]
    )
    cos_two, sin_two = cos_sin(highs, second_len, second_len)
    table_two = jnp.stack(
        [jnp.stack([cos_two, sin_two], axis=1), jnp.stack([-sin_two, cos_two], axis=1)]
    )
    return jnp.einsum("yqxb,xmcb->yqmc", table_two, twisted, precision=precision)


def correlate(own, gathered, prior, scale):
    _, groups_inp, groups_tm, count_s, inputs, lanes = own.shape
    rows = groups_inp * inputs
    cols = gathered.shape[1] * gathered.shape[4]
    depth = groups_tm * lanes
    out_groups = lanes // CH_AVG

    def kernel(*refs):
        own_ref, gat_ref = refs[0], refs[1]
        out_ref = refs[-1]
        spectrum = pl.program_id(0)

        def chunks(ref, part):
            pieces = [ref[part, :, t, 0].reshape(-1, lanes) for t in range(groups_tm)]
            return jnp.concatenate(pieces, axis=1)

        x0, x1 = chunks(own_ref, 0), chunks(own_ref, 1)
        c0, c1 = chunks(gat_ref, 0), chunks(gat_ref, 1)
        low = (lax.broadcasted_iota(jnp.int32, (1, depth), 1) % lanes) < CH_AVG

        def near(value, upper):
            return pltpu.roll(value, depth - CH_AVG if upper else CH_AVG, 1)

        def products(upper):
            if upper:
                left_re = jnp.where(low, near(x0, True), x1)
                left_im = jnp.where(low, near(x1, True), -x0)
                right = jnp.where(low, near(c0, True), c1)
            else:
                left_re = jnp.where(low, x0, near(x1, False))
                left_im = jnp.where(low, x1, -near(x0, False))
                right = jnp.where(low, c0, near(c1, False))
            dims = (((1,), (1,)), ((), ()))
            real = lax.dot_general(left_re, right, dims, preferred_element_type=jnp.float32)
            imag = lax.dot_general(left_im, right, dims, preferred_element_type=jnp.float32)
            return real * scale, imag * scale

        for g in range(out_groups):
            real, imag = products(g == 1)

            @pl.when(spectrum == 0)
            def _():
                if prior is None:
                    out_ref[0, g] = real
                    out_ref[1, g] = imag
                else:
                    out_ref[0, g] = refs[2][0, g] + real
                    out_ref[1, g] = refs[2][1, g] + imag

            @pl.when(spectrum != 0)
            def _():
                out_ref[0, g] += real
                out_ref[1, g] += imag

    block_own = (2, groups_inp, groups_tm, 1, inputs, lanes)
    block_gat = (2, groups_inp, groups_tm, 1, gathered.shape[4], lanes)
    out_block = (2, out_groups, rows, cols)
    in_specs = [
        pl.BlockSpec(block_own, lambda s: (0, 0, 0, s, 0, 0)),
        pl.BlockSpec(block_gat, lambda s: (0, 0, 0, s, 0, 0)),
    ]
    operands = [own, gathered]
    aliases = {}
    if prior is not None:
        in_specs.append(pl.BlockSpec(out_block, lambda s: (0, 0, 0, 0), pipeline_mode=pl.Buffered(1)))
        operands.append(prior)
        aliases = {2: 0}
    flops = 2 * 2 * rows * cols * depth * count_s * out_groups
    return pl.pallas_call(
        kernel,
        grid=(count_s,),
        in_specs=in_specs,
        out_specs=pl.BlockSpec(out_block, lambda s: (0, 0, 0, 0)),
        out_shape=jax.ShapeDtypeStruct((2, out_groups, rows, cols), jnp.float32),
        input_output_aliases=aliases,
        compiler_params=pltpu.CompilerParams(vmem_limit_bytes=64 * 1000 * 1000),
        cost_estimate=pl.CostEstimate(
            flops=flops, transcendentals=0, bytes_accessed=2 * (own.size + gathered.size) + 8 * rows * cols * out_groups
        ),
    )(*operands)


def shards(voltages, taps, flags):
    inputs = voltages.shape[0]
    tap_count = taps.shape[0]
    length = taps.shape[1]
    second_len = length // FIRST
    spectra_dev = voltages.shape[1] // length
    reach = tap_count - 1
    local = spectra_dev - reach
    precision = lax.Precision.HIGH
    blocked = voltages.reshape(inputs, spectra_dev, FIRST, second_len)
    assert spectra_dev >= tap_count and reach >= 2
    ahead = reach - 1
    leading = voltages[:, : ahead * length].astype(jnp.bfloat16)
    following = passed_along(leading, "tm", -1).reshape(inputs, ahead, FIRST, second_len)
    blocks_tm = lax.axis_size("tm")
    trailing = voltages[:, (spectra_dev - 1) * length :].astype(jnp.bfloat16)
    previous = lax.ppermute(
        trailing, "tm", [(source, (source + 1) % blocks_tm) for source in range(blocks_tm)]
    ).reshape(inputs, FIRST, second_len)
    samples = lax.optimization_barrier(blocked).astype(jnp.float32)
    tap_blocks = taps.reshape(tap_count, FIRST, second_len)

    def filtered(pieces, count):
        rows = []
        for spectrum in range(count):
            total = jnp.zeros((inputs, FIRST, second_len), jnp.float32)
            for offset in range(tap_count):
                total = total + tap_blocks[offset][None] * pieces[spectrum + offset]
            rows.append(total)
        return jnp.concatenate(rows, axis=0)

    scale = flags.astype(jnp.float32) / (8.0 * math.sqrt(length))
    groups_inp = lax.axis_size("inp")
    groups_tm = lax.axis_size("tm")
    count = float(groups_tm * spectra_dev * CH_AVG)

    def corner_turn(parts, count_s):
        spectra = (parts * jnp.tile(scale, count_s)[None, None, :, None]).astype(jnp.bfloat16)
        turned = lax.all_to_all(spectra, ("inp", "tm"), split_axis=1, concat_axis=1, tiled=True)
        own = turned.reshape(2, groups_inp, groups_tm, count_s, inputs, FIRST)
        return own, lax.all_gather(own, "bl", axis=4, tiled=True)

    own_pieces = [samples[:, j] for j in range(spectra_dev)]
    keep = (lax.axis_index("tm") != 0).astype(jnp.float32)
    wrapped = [previous.astype(jnp.float32)] + [piece * keep for piece in own_pieces[:reach]]
    first_part = transform(filtered(own_pieces, 1), length, precision)
    own, gathered = corner_turn(first_part, 1)
    visibilities = correlate(own, gathered, None, 1.0 / count)
    next_pieces = [following[:, j].astype(jnp.float32) for j in range(ahead)]
    later = spectra_dev - 2
    rest = own_pieces[1:] + next_pieces
    second_part = jnp.concatenate(
        [transform(filtered(wrapped, 1), length, precision)]
        + [transform(filtered(rest[j:], 1), length, precision) for j in range(later)],
        axis=2,
    )
    own, gathered = corner_turn(second_part, later + 1)
    visibilities = correlate(own, gathered, visibilities, 1.0 / count)
    return visibilities.reshape(2, FIRST // CH_AVG, groups_inp, inputs, -1)


def solution(mesh):
    in_specs = (P(("inp", "bl"), "tm"), P(), P(("inp", "bl")))
    out_specs = P(None, ("inp", "tm"), None, "bl", None)
    return jax.shard_map(shards, mesh=mesh, in_specs=in_specs, out_specs=out_specs, check_vma=False)
```

```python
import math

import jax
import jax.numpy as jnp
from jax import lax
from jax.experimental import pallas as pl
from jax.experimental.pallas import tpu as pltpu
from jax.sharding import PartitionSpec as P

CH_AVG = 64
FIRST = 128


def passed_along(value, axis, steps):
    count = lax.axis_size(axis)
    initial, last = (max(0, -steps), min(count, count - steps))
    return lax.ppermute(value, axis, [(source, source + steps) for source in range(initial, last)])


def cos_sin(height, breadth, period):
    grid = lax.broadcasted_iota(jnp.int32, (height, breadth), 0) * lax.broadcasted_iota(
        jnp.int32, (height, breadth), 1
    )
    angle = (grid % period).astype(jnp.float32) * (2.0 * math.pi / period)
    return (jnp.cos(angle), jnp.sin(angle))


def transform(blocks, length, precision):
    first_len = FIRST
    second_len = length // first_len
    highs = length // 2 // first_len
    cos_one, sin_one = cos_sin(first_len, first_len, first_len)
    table_one = jnp.stack([cos_one, -sin_one])
    section_one = jnp.einsum("xca,mab->xmcb", table_one, blocks, precision=precision)
    cos_twist, sin_twist = cos_sin(first_len, second_len, length)
    real_one = section_one[0]
    imag_one = section_one[1]
    twisted = jnp.stack(
        [real_one * cos_twist + imag_one * sin_twist, imag_one * cos_twist - real_one * sin_twist]
    )
    cos_two, sin_two = cos_sin(highs, second_len, second_len)
    table_two = jnp.stack(
        [jnp.stack([cos_two, sin_two], axis=1), jnp.stack([-sin_two, cos_two], axis=1)]
    )
    return jnp.einsum("yqxb,xmcb->yqmc", table_two, twisted, precision=precision)


def correlate(own, gathered, prior, scale):
    _, groups_inp, groups_tm, count_s, inputs, lanes = own.shape
    rows = groups_inp * inputs
    cols = gathered.shape[1] * gathered.shape[4]
    depth = groups_tm * lanes
    out_groups = lanes // CH_AVG

    def kernel(*refs):
        own_ref, gat_ref = refs[0], refs[1]
        out_ref = refs[-1]
        spectrum = pl.program_id(0)

        def chunks(ref, part):
            pieces = [ref[part, :, t, 0].reshape(-1, lanes) for t in range(groups_tm)]
            return jnp.concatenate(pieces, axis=1)

        x0, x1 = chunks(own_ref, 0), chunks(own_ref, 1)
        c0, c1 = chunks(gat_ref, 0), chunks(gat_ref, 1)
        low = (lax.broadcasted_iota(jnp.int32, (1, depth), 1) % lanes) < CH_AVG

        def near(value, upper):
            return pltpu.roll(value, depth - CH_AVG if upper else CH_AVG, 1)

        def products(upper):
            if upper:
                left_re = jnp.where(low, near(x0, True), x1)
                left_im = jnp.where(low, near(x1, True), -x0)
                right = jnp.where(low, near(c0, True), c1)
            else:
                left_re = jnp.where(low, x0, near(x1, False))
                left_im = jnp.where(low, x1, -near(x0, False))
                right = jnp.where(low, c0, near(c1, False))
            dims = (((1,), (1,)), ((), ()))
            left = jnp.concatenate([left_re, left_im], axis=0)
            both = lax.dot_general(left, right, dims, preferred_element_type=jnp.float32) * scale
            return both[:rows], both[rows:]

        for g in range(out_groups):
            real, imag = products(g == 1)

            @pl.when(spectrum == 0)
            def _():
                if prior is None:
                    out_ref[0, g] = real
                    out_ref[1, g] = imag
                else:
                    out_ref[0, g] = refs[2][0, g] + real
                    out_ref[1, g] = refs[2][1, g] + imag

            @pl.when(spectrum != 0)
            def _():
                out_ref[0, g] += real
                out_ref[1, g] += imag

    block_own = (2, groups_inp, groups_tm, 1, inputs, lanes)
    block_gat = (2, groups_inp, groups_tm, 1, gathered.shape[4], lanes)
    out_block = (2, out_groups, rows, cols)
    in_specs = [
        pl.BlockSpec(block_own, lambda s: (0, 0, 0, s, 0, 0)),
        pl.BlockSpec(block_gat, lambda s: (0, 0, 0, s, 0, 0)),
    ]
    operands = [own, gathered]
    aliases = {}
    if prior is not None:
        in_specs.append(pl.BlockSpec(out_block, lambda s: (0, 0, 0, 0), pipeline_mode=pl.Buffered(1)))
        operands.append(prior)
        aliases = {2: 0}
    flops = 2 * 2 * rows * cols * depth * count_s * out_groups
    return pl.pallas_call(
        kernel,
        grid=(count_s,),
        in_specs=in_specs,
        out_specs=pl.BlockSpec(out_block, lambda s: (0, 0, 0, 0)),
        out_shape=jax.ShapeDtypeStruct((2, out_groups, rows, cols), jnp.float32),
        input_output_aliases=aliases,
        compiler_params=pltpu.CompilerParams(vmem_limit_bytes=64 * 1000 * 1000),
        cost_estimate=pl.CostEstimate(
            flops=flops, transcendentals=0, bytes_accessed=2 * (own.size + gathered.size) + 8 * rows * cols * out_groups
        ),
    )(*operands)


def shards(voltages, taps, flags):
    inputs = voltages.shape[0]
    tap_count = taps.shape[0]
    length = taps.shape[1]
    second_len = length // FIRST
    spectra_dev = voltages.shape[1] // length
    reach = tap_count - 1
    local = spectra_dev - reach
    precision = lax.Precision.HIGH
    blocked = voltages.reshape(inputs, spectra_dev, FIRST, second_len)
    assert spectra_dev >= tap_count and reach >= 2
    ahead = reach - 1
    leading = voltages[:, : ahead * length].astype(jnp.bfloat16)
    following = passed_along(leading, "tm", -1).reshape(inputs, ahead, FIRST, second_len)
    blocks_tm = lax.axis_size("tm")
    trailing = voltages[:, (spectra_dev - 1) * length :].astype(jnp.bfloat16)
    previous = lax.ppermute(
        trailing, "tm", [(source, (source + 1) % blocks_tm) for source in range(blocks_tm)]
    ).reshape(inputs, FIRST, second_len)
    samples = lax.optimization_barrier(blocked).astype(jnp.float32)
    tap_blocks = taps.reshape(tap_count, FIRST, second_len)

    def filtered(pieces, count):
        rows = []
        for spectrum in range(count):
            total = jnp.zeros((inputs, FIRST, second_len), jnp.float32)
            for offset in range(tap_count):
                total = total + tap_blocks[offset][None] * pieces[spectrum + offset]
            rows.append(total)
        return jnp.concatenate(rows, axis=0)

    scale = flags.astype(jnp.float32) / (8.0 * math.sqrt(length))
    groups_inp = lax.axis_size("inp")
    groups_tm = lax.axis_size("tm")
    count = float(groups_tm * spectra_dev * CH_AVG)

    def corner_turn(parts, count_s):
        spectra = (parts * jnp.tile(scale, count_s)[None, None, :, None]).astype(jnp.bfloat16)
        turned = lax.all_to_all(spectra, ("inp", "tm"), split_axis=1, concat_axis=1, tiled=True)
        own = turned.reshape(2, groups_inp, groups_tm, count_s, inputs, FIRST)
        return own, lax.all_gather(own, "bl", axis=4, tiled=True)

    own_pieces = [samples[:, j] for j in range(spectra_dev)]
    keep = (lax.axis_index("tm") != 0).astype(jnp.float32)
    wrapped = [previous.astype(jnp.float32)] + [piece * keep for piece in own_pieces[:reach]]
    first_part = transform(filtered(own_pieces, 1), length, precision)
    own, gathered = corner_turn(first_part, 1)
    visibilities = correlate(own, gathered, None, 1.0 / count)
    next_pieces = [following[:, j].astype(jnp.float32) for j in range(ahead)]
    later = spectra_dev - 2
    rest = own_pieces[1:] + next_pieces
    second_part = jnp.concatenate(
        [transform(filtered(wrapped, 1), length, precision)]
        + [transform(filtered(rest[j:], 1), length, precision) for j in range(later)],
        axis=2,
    )
    own, gathered = corner_turn(second_part, later + 1)
    visibilities = correlate(own, gathered, visibilities, 1.0 / count)
    return visibilities.reshape(2, FIRST // CH_AVG, groups_inp, inputs, -1)


def solution(mesh):
    in_specs = (P(("inp", "bl"), "tm"), P(), P(("inp", "bl")))
    out_specs = P(None, ("inp", "tm"), None, "bl", None)
    return jax.shard_map(shards, mesh=mesh, in_specs=in_specs, out_specs=out_specs, check_vma=False)
```

```python
import math

import jax
import jax.numpy as jnp
from jax import lax
from jax.experimental import pallas as pl
from jax.experimental.pallas import tpu as pltpu
from jax.sharding import PartitionSpec as P

CH_AVG = 64
FIRST = 128


def passed_along(value, axis, steps):
    count = lax.axis_size(axis)
    initial, last = (max(0, -steps), min(count, count - steps))
    return lax.ppermute(value, axis, [(source, source + steps) for source in range(initial, last)])


def cos_sin(height, breadth, period):
    grid = lax.broadcasted_iota(jnp.int32, (height, breadth), 0) * lax.broadcasted_iota(
        jnp.int32, (height, breadth), 1
    )
    angle = (grid % period).astype(jnp.float32) * (2.0 * math.pi / period)
    return (jnp.cos(angle), jnp.sin(angle))


def transform(blocks, length, precision):
    first_len = FIRST
    second_len = length // first_len
    highs = length // 2 // first_len
    cos_one, sin_one = cos_sin(first_len, first_len, first_len)
    table_one = jnp.stack([cos_one, -sin_one])
    section_one = jnp.einsum("xca,mab->xmcb", table_one, blocks, precision=precision)
    cos_twist, sin_twist = cos_sin(first_len, second_len, length)
    real_one = section_one[0]
    imag_one = section_one[1]
    twisted = jnp.stack(
        [real_one * cos_twist + imag_one * sin_twist, imag_one * cos_twist - real_one * sin_twist]
    )
    cos_two, sin_two = cos_sin(highs, second_len, second_len)
    table_two = jnp.stack(
        [jnp.stack([cos_two, sin_two], axis=1), jnp.stack([-sin_two, cos_two], axis=1)]
    )
    return jnp.einsum("yqxb,xmcb->yqmc", table_two, twisted, precision=precision)


def correlate(own, gathered, prior, scale):
    _, groups_inp, groups_tm, count_s, inputs, lanes = own.shape
    rows = groups_inp * inputs
    cols = gathered.shape[1] * gathered.shape[4]
    depth = groups_tm * lanes
    out_groups = lanes // CH_AVG

    def kernel(*refs):
        own_ref, gat_ref = refs[0], refs[1]
        out_ref = refs[-1]
        spectrum = pl.program_id(0)

        def chunks(ref, part):
            pieces = [ref[part, :, t, 0].reshape(-1, lanes) for t in range(groups_tm)]
            return jnp.concatenate(pieces, axis=1)

        x0, x1 = chunks(own_ref, 0), chunks(own_ref, 1)
        c0, c1 = chunks(gat_ref, 0), chunks(gat_ref, 1)
        low = (lax.broadcasted_iota(jnp.int32, (1, depth), 1) % lanes) < CH_AVG

        right = jnp.concatenate([c0, c1], axis=1)

        def products(upper):
            mask = (low != upper).astype(x0.dtype)
            m0, m1 = x0 * mask, x1 * mask
            left = jnp.concatenate(
                [jnp.concatenate([m0, m1], axis=1), jnp.concatenate([m1, -m0], axis=1)], axis=0
            )
            dims = (((1,), (1,)), ((), ()))
            both = lax.dot_general(left, right, dims, preferred_element_type=jnp.float32) * scale
            return both[:rows], both[rows:]

        for g in range(out_groups):
            real, imag = products(g == 1)

            @pl.when(spectrum == 0)
            def _():
                if prior is None:
                    out_ref[0, g] = real
                    out_ref[1, g] = imag
                else:
                    out_ref[0, g] = refs[2][0, g] + real
                    out_ref[1, g] = refs[2][1, g] + imag

            @pl.when(spectrum != 0)
            def _():
                out_ref[0, g] += real
                out_ref[1, g] += imag

    block_own = (2, groups_inp, groups_tm, 1, inputs, lanes)
    block_gat = (2, groups_inp, groups_tm, 1, gathered.shape[4], lanes)
    out_block = (2, out_groups, rows, cols)
    in_specs = [
        pl.BlockSpec(block_own, lambda s: (0, 0, 0, s, 0, 0)),
        pl.BlockSpec(block_gat, lambda s: (0, 0, 0, s, 0, 0)),
    ]
    operands = [own, gathered]
    aliases = {}
    if prior is not None:
        in_specs.append(pl.BlockSpec(out_block, lambda s: (0, 0, 0, 0), pipeline_mode=pl.Buffered(1)))
        operands.append(prior)
        aliases = {2: 0}
    flops = 2 * 2 * rows * cols * depth * count_s * out_groups
    return pl.pallas_call(
        kernel,
        grid=(count_s,),
        in_specs=in_specs,
        out_specs=pl.BlockSpec(out_block, lambda s: (0, 0, 0, 0)),
        out_shape=jax.ShapeDtypeStruct((2, out_groups, rows, cols), jnp.float32),
        input_output_aliases=aliases,
        compiler_params=pltpu.CompilerParams(vmem_limit_bytes=64 * 1000 * 1000),
        cost_estimate=pl.CostEstimate(
            flops=flops, transcendentals=0, bytes_accessed=2 * (own.size + gathered.size) + 8 * rows * cols * out_groups
        ),
    )(*operands)


def shards(voltages, taps, flags):
    inputs = voltages.shape[0]
    tap_count = taps.shape[0]
    length = taps.shape[1]
    second_len = length // FIRST
    spectra_dev = voltages.shape[1] // length
    reach = tap_count - 1
    local = spectra_dev - reach
    precision = lax.Precision.HIGH
    blocked = voltages.reshape(inputs, spectra_dev, FIRST, second_len)
    assert spectra_dev >= tap_count and reach >= 2
    ahead = reach - 1
    leading = voltages[:, : ahead * length].astype(jnp.bfloat16)
    following = passed_along(leading, "tm", -1).reshape(inputs, ahead, FIRST, second_len)
    blocks_tm = lax.axis_size("tm")
    trailing = voltages[:, (spectra_dev - 1) * length :].astype(jnp.bfloat16)
    previous = lax.ppermute(
        trailing, "tm", [(source, (source + 1) % blocks_tm) for source in range(blocks_tm)]
    ).reshape(inputs, FIRST, second_len)
    samples = lax.optimization_barrier(blocked).astype(jnp.float32)
    tap_blocks = taps.reshape(tap_count, FIRST, second_len)

    def filtered(pieces, count):
        rows = []
        for spectrum in range(count):
            total = jnp.zeros((inputs, FIRST, second_len), jnp.float32)
            for offset in range(tap_count):
                total = total + tap_blocks[offset][None] * pieces[spectrum + offset]
            rows.append(total)
        return jnp.concatenate(rows, axis=0)

    scale = flags.astype(jnp.float32) / (8.0 * math.sqrt(length))
    groups_inp = lax.axis_size("inp")
    groups_tm = lax.axis_size("tm")
    count = float(groups_tm * spectra_dev * CH_AVG)

    def corner_turn(parts, count_s):
        spectra = (parts * jnp.tile(scale, count_s)[None, None, :, None]).astype(jnp.bfloat16)
        turned = lax.all_to_all(spectra, ("inp", "tm"), split_axis=1, concat_axis=1, tiled=True)
        own = turned.reshape(2, groups_inp, groups_tm, count_s, inputs, FIRST)
        return own, lax.all_gather(own, "bl", axis=4, tiled=True)

    own_pieces = [samples[:, j] for j in range(spectra_dev)]
    keep = (lax.axis_index("tm") != 0).astype(jnp.float32)
    wrapped = [previous.astype(jnp.float32)] + [piece * keep for piece in own_pieces[:reach]]
    first_part = transform(filtered(own_pieces, 1), length, precision)
    own, gathered = corner_turn(first_part, 1)
    visibilities = correlate(own, gathered, None, 1.0 / count)
    next_pieces = [following[:, j].astype(jnp.float32) for j in range(ahead)]
    later = spectra_dev - 2
    rest = own_pieces[1:] + next_pieces
    second_part = jnp.concatenate(
        [transform(filtered(wrapped, 1), length, precision)]
        + [transform(filtered(rest[j:], 1), length, precision) for j in range(later)],
        axis=2,
    )
    own, gathered = corner_turn(second_part, later + 1)
    visibilities = correlate(own, gathered, visibilities, 1.0 / count)
    return visibilities.reshape(2, FIRST // CH_AVG, groups_inp, inputs, -1)


def solution(mesh):
    in_specs = (P(("inp", "bl"), "tm"), P(), P(("inp", "bl")))
    out_specs = P(None, ("inp", "tm"), None, "bl", None)
    return jax.shard_map(shards, mesh=mesh, in_specs=in_specs, out_specs=out_specs, check_vma=False)
```

```python
import math

import jax
import jax.numpy as jnp
from jax import lax
from jax.experimental import pallas as pl
from jax.experimental.pallas import tpu as pltpu
from jax.sharding import PartitionSpec as P

CH_AVG = 64
FIRST = 128


def passed_along(value, axis, steps):
    count = lax.axis_size(axis)
    initial, last = (max(0, -steps), min(count, count - steps))
    return lax.ppermute(value, axis, [(source, source + steps) for source in range(initial, last)])


def cos_sin(height, breadth, period):
    grid = lax.broadcasted_iota(jnp.int32, (height, breadth), 0) * lax.broadcasted_iota(
        jnp.int32, (height, breadth), 1
    )
    angle = (grid % period).astype(jnp.float32) * (2.0 * math.pi / period)
    return (jnp.cos(angle), jnp.sin(angle))


def transform(blocks, length, precision):
    first_len = FIRST
    second_len = length // first_len
    highs = length // 2 // first_len
    cos_one, sin_one = cos_sin(first_len, first_len, first_len)
    table_one = jnp.stack([cos_one, -sin_one])
    section_one = jnp.einsum("xca,mab->xmcb", table_one, blocks, precision=precision)
    cos_twist, sin_twist = cos_sin(first_len, second_len, length)
    real_one = section_one[0]
    imag_one = section_one[1]
    twisted = jnp.stack(
        [real_one * cos_twist + imag_one * sin_twist, imag_one * cos_twist - real_one * sin_twist]
    )
    cos_two, sin_two = cos_sin(highs, second_len, second_len)
    table_two = jnp.stack(
        [jnp.stack([cos_two, sin_two], axis=1), jnp.stack([-sin_two, cos_two], axis=1)]
    )
    return jnp.einsum("yqxb,xmcb->yqmc", table_two, twisted, precision=precision)


def correlate(own, gathered, prior, scale):
    _, groups_inp, groups_tm, count_s, inputs, lanes = own.shape
    rows = groups_inp * inputs
    cols = gathered.shape[1] * gathered.shape[4]
    depth = groups_tm * lanes
    out_groups = lanes // CH_AVG

    def kernel(*refs):
        own_ref, gat_ref = refs[0], refs[1]
        out_ref = refs[-1]
        group = pl.program_id(0)
        spectrum = pl.program_id(1)

        @pl.when(spectrum == 0)
        def _():
            if prior is None:
                out_ref[...] = jnp.zeros(out_ref.shape, out_ref.dtype)
            else:
                out_ref[...] = refs[2][...]

        def chunks(ref, part):
            pieces = [ref[part, :, t, 0].reshape(-1, lanes) for t in range(groups_tm)]
            return jnp.concatenate(pieces, axis=1)

        x0, x1 = chunks(own_ref, 0), chunks(own_ref, 1)
        c0, c1 = chunks(gat_ref, 0), chunks(gat_ref, 1)
        low = (lax.broadcasted_iota(jnp.int32, (1, depth), 1) % lanes) < CH_AVG

        def near(value, upper):
            return pltpu.roll(value, depth - CH_AVG if upper else CH_AVG, 1)

        def accumulate(upper):
            if upper:
                left_re = jnp.where(low, near(x0, True), x1)
                left_im = jnp.where(low, near(x1, True), -x0)
                right = jnp.where(low, near(c0, True), c1)
            else:
                left_re = jnp.where(low, x0, near(x1, False))
                left_im = jnp.where(low, x1, -near(x0, False))
                right = jnp.where(low, c0, near(c1, False))
            dims = (((1,), (1,)), ((), ()))
            real = lax.dot_general(left_re, right, dims, preferred_element_type=jnp.float32)
            imag = lax.dot_general(left_im, right, dims, preferred_element_type=jnp.float32)
            out_ref[0, 0] += real * scale
            out_ref[1, 0] += imag * scale

        for g in range(out_groups):
            pl.when(group == g)(lambda g=g: accumulate(g == 1))

    block_own = (2, groups_inp, groups_tm, 1, inputs, lanes)
    block_gat = (2, groups_inp, groups_tm, 1, gathered.shape[4], lanes)
    out_block = (2, 1, rows, cols)
    in_specs = [
        pl.BlockSpec(block_own, lambda g, s: (0, 0, 0, s, 0, 0)),
        pl.BlockSpec(block_gat, lambda g, s: (0, 0, 0, s, 0, 0)),
    ]
    operands = [own, gathered]
    aliases = {}
    if prior is not None:
        in_specs.append(pl.BlockSpec(out_block, lambda g, s: (0, g, 0, 0)))
        operands.append(prior)
        aliases = {2: 0}
    flops = 2 * 2 * rows * cols * depth * count_s * out_groups
    return pl.pallas_call(
        kernel,
        grid=(out_groups, count_s),
        in_specs=in_specs,
        out_specs=pl.BlockSpec(out_block, lambda g, s: (0, g, 0, 0)),
        out_shape=jax.ShapeDtypeStruct((2, out_groups, rows, cols), jnp.float32),
        input_output_aliases=aliases,
        compiler_params=pltpu.CompilerParams(vmem_limit_bytes=60 * 1024 * 1024),
        cost_estimate=pl.CostEstimate(
            flops=flops, transcendentals=0, bytes_accessed=2 * (own.size + gathered.size) * out_groups + 8 * rows * cols * out_groups
        ),
    )(*operands)


def shards(voltages, taps, flags):
    inputs = voltages.shape[0]
    tap_count = taps.shape[0]
    length = taps.shape[1]
    second_len = length // FIRST
    spectra_dev = voltages.shape[1] // length
    reach = tap_count - 1
    local = spectra_dev - reach
    precision = lax.Precision.HIGH
    blocked = voltages.reshape(inputs, spectra_dev, FIRST, second_len)
    assert spectra_dev >= tap_count and reach >= 2
    ahead = reach - 1
    leading = voltages[:, : ahead * length].astype(jnp.bfloat16)
    following = passed_along(leading, "tm", -1).reshape(inputs, ahead, FIRST, second_len)
    blocks_tm = lax.axis_size("tm")
    trailing = voltages[:, (spectra_dev - 1) * length :].astype(jnp.bfloat16)
    previous = lax.ppermute(
        trailing, "tm", [(source, (source + 1) % blocks_tm) for source in range(blocks_tm)]
    ).reshape(inputs, FIRST, second_len)
    samples = lax.optimization_barrier(blocked).astype(jnp.float32)
    tap_blocks = taps.reshape(tap_count, FIRST, second_len)

    def filtered(pieces, count):
        rows = []
        for spectrum in range(count):
            total = jnp.zeros((inputs, FIRST, second_len), jnp.float32)
            for offset in range(tap_count):
                total = total + tap_blocks[offset][None] * pieces[spectrum + offset]
            rows.append(total)
        return jnp.concatenate(rows, axis=0)

    scale = flags.astype(jnp.float32) / (8.0 * math.sqrt(length))
    groups_inp = lax.axis_size("inp")
    groups_tm = lax.axis_size("tm")
    count = float(groups_tm * spectra_dev * CH_AVG)

    def corner_turn(parts, count_s, swap=False):
        spectra = (parts * jnp.tile(scale, count_s)[None, None, :, None]).astype(jnp.bfloat16)
        turned = lax.all_to_all(spectra, ("inp", "tm"), split_axis=1, concat_axis=1, tiled=True)
        own = turned.reshape(2, groups_inp, groups_tm, count_s, inputs, FIRST)
        if not swap:
            return own, lax.all_gather(own, "bl", axis=4, tiled=True)
        other = lax.ppermute(own, "bl", [(0, 1), (1, 0)])
        first = lax.axis_index("bl") == 0
        lower = jnp.where(first, own, other)
        upper = jnp.where(first, other, own)
        return own, jnp.concatenate([lower, upper], axis=4)

    own_pieces = [samples[:, j] for j in range(spectra_dev)]
    keep = (lax.axis_index("tm") != 0).astype(jnp.float32)
    wrapped = [previous.astype(jnp.float32)] + [piece * keep for piece in own_pieces[:reach]]
    first_part = transform(filtered(own_pieces, 1), length, precision)
    own, gathered = corner_turn(first_part, 1)
    visibilities = correlate(own, gathered, None, 1.0 / count)
    next_pieces = [following[:, j].astype(jnp.float32) for j in range(ahead)]
    later = spectra_dev - 2
    rest = own_pieces[1:] + next_pieces
    second_part = jnp.concatenate(
        [transform(filtered(wrapped, 1), length, precision)]
        + [transform(filtered(rest[j:], 1), length, precision) for j in range(later)],
        axis=2,
    )
    own, gathered = corner_turn(second_part, later + 1, swap=True)
    visibilities = correlate(own, gathered, visibilities, 1.0 / count)
    return visibilities.reshape(2, FIRST // CH_AVG, groups_inp, inputs, -1)


def solution(mesh):
    in_specs = (P(("inp", "bl"), "tm"), P(), P(("inp", "bl")))
    out_specs = P(None, ("inp", "tm"), None, "bl", None)
    return jax.shard_map(shards, mesh=mesh, in_specs=in_specs, out_specs=out_specs, check_vma=False)
```

```python
import math

import jax
import jax.numpy as jnp
from jax import lax
from jax.experimental import pallas as pl
from jax.experimental.pallas import tpu as pltpu
from jax.sharding import PartitionSpec as P

CH_AVG = 64
FIRST = 128


def passed_along(value, axis, steps):
    count = lax.axis_size(axis)
    initial, last = (max(0, -steps), min(count, count - steps))
    return lax.ppermute(value, axis, [(source, source + steps) for source in range(initial, last)])


def cos_sin(height, breadth, period):
    grid = lax.broadcasted_iota(jnp.int32, (height, breadth), 0) * lax.broadcasted_iota(
        jnp.int32, (height, breadth), 1
    )
    angle = (grid % period).astype(jnp.float32) * (2.0 * math.pi / period)
    return (jnp.cos(angle), jnp.sin(angle))


def transform(blocks, length, precision):
    first_len = FIRST
    second_len = length // first_len
    highs = length // 2 // first_len
    cos_one, sin_one = cos_sin(first_len, first_len, first_len)
    table_one = jnp.stack([cos_one, -sin_one])
    section_one = jnp.einsum("xca,mab->xmcb", table_one, blocks, precision=precision)
    cos_twist, sin_twist = cos_sin(first_len, second_len, length)
    real_one = section_one[0]
    imag_one = section_one[1]
    twisted = jnp.stack(
        [real_one * cos_twist + imag_one * sin_twist, imag_one * cos_twist - real_one * sin_twist]
    )
    cos_two, sin_two = cos_sin(highs, second_len, second_len)
    table_two = jnp.stack(
        [jnp.stack([cos_two, sin_two], axis=1), jnp.stack([-sin_two, cos_two], axis=1)]
    )
    return jnp.einsum("yqxb,xmcb->yqmc", table_two, twisted, precision=precision)


def correlate(own, gathered, prior, scale):
    groups_inp, groups_tm, _, count_s, inputs, lanes = own.shape
    rows = groups_inp * inputs
    cols = gathered.shape[0] * gathered.shape[4]
    depth = groups_tm * lanes
    out_groups = lanes // CH_AVG

    def kernel(*refs):
        own_ref, gat_ref = refs[0], refs[1]
        out_ref = refs[-1]
        group = pl.program_id(0)
        spectrum = pl.program_id(1)

        @pl.when(spectrum == 0)
        def _():
            if prior is None:
                out_ref[...] = jnp.zeros(out_ref.shape, out_ref.dtype)
            else:
                out_ref[...] = refs[2][...]

        def chunks(ref, part):
            pieces = [ref[:, t, part, 0].reshape(-1, lanes) for t in range(groups_tm)]
            return jnp.concatenate(pieces, axis=1)

        x0, x1 = chunks(own_ref, 0), chunks(own_ref, 1)
        c0, c1 = chunks(gat_ref, 0), chunks(gat_ref, 1)
        low = (lax.broadcasted_iota(jnp.int32, (1, depth), 1) % lanes) < CH_AVG

        def near(value, upper):
            return pltpu.roll(value, depth - CH_AVG if upper else CH_AVG, 1)

        def accumulate(upper):
            if upper:
                left_re = jnp.where(low, near(x0, True), x1)
                left_im = jnp.where(low, near(x1, True), -x0)
                right = jnp.where(low, near(c0, True), c1)
            else:
                left_re = jnp.where(low, x0, near(x1, False))
                left_im = jnp.where(low, x1, -near(x0, False))
                right = jnp.where(low, c0, near(c1, False))
            dims = (((1,), (1,)), ((), ()))
            real = lax.dot_general(left_re, right, dims, preferred_element_type=jnp.float32)
            imag = lax.dot_general(left_im, right, dims, preferred_element_type=jnp.float32)
            out_ref[0, 0] += real * scale
            out_ref[1, 0] += imag * scale

        for g in range(out_groups):
            pl.when(group == g)(lambda g=g: accumulate(g == 1))

    block_own = (groups_inp, groups_tm, 2, 1, inputs, lanes)
    block_gat = (groups_inp, groups_tm, 2, 1, gathered.shape[4], lanes)
    out_block = (2, 1, rows, cols)
    in_specs = [
        pl.BlockSpec(block_own, lambda g, s: (0, 0, 0, s, 0, 0)),
        pl.BlockSpec(block_gat, lambda g, s: (0, 0, 0, s, 0, 0)),
    ]
    operands = [own, gathered]
    aliases = {}
    if prior is not None:
        in_specs.append(pl.BlockSpec(out_block, lambda g, s: (0, g, 0, 0)))
        operands.append(prior)
        aliases = {2: 0}
    flops = 2 * 2 * rows * cols * depth * count_s * out_groups
    return pl.pallas_call(
        kernel,
        grid=(out_groups, count_s),
        in_specs=in_specs,
        out_specs=pl.BlockSpec(out_block, lambda g, s: (0, g, 0, 0)),
        out_shape=jax.ShapeDtypeStruct((2, out_groups, rows, cols), jnp.float32),
        input_output_aliases=aliases,
        compiler_params=pltpu.CompilerParams(vmem_limit_bytes=60 * 1024 * 1024),
        cost_estimate=pl.CostEstimate(
            flops=flops, transcendentals=0, bytes_accessed=2 * (own.size + gathered.size) * out_groups + 8 * rows * cols * out_groups
        ),
    )(*operands)


def shards(voltages, taps, flags):
    inputs = voltages.shape[0]
    tap_count = taps.shape[0]
    length = taps.shape[1]
    second_len = length // FIRST
    spectra_dev = voltages.shape[1] // length
    reach = tap_count - 1
    local = spectra_dev - reach
    precision = lax.Precision.HIGH
    blocked = voltages.reshape(inputs, spectra_dev, FIRST, second_len)
    assert spectra_dev >= tap_count and reach >= 2
    ahead = reach - 1
    leading = voltages[:, : ahead * length].astype(jnp.bfloat16)
    following = passed_along(leading, "tm", -1).reshape(inputs, ahead, FIRST, second_len)
    blocks_tm = lax.axis_size("tm")
    trailing = voltages[:, (spectra_dev - 1) * length :].astype(jnp.bfloat16)
    previous = lax.ppermute(
        trailing, "tm", [(source, (source + 1) % blocks_tm) for source in range(blocks_tm)]
    ).reshape(inputs, FIRST, second_len)
    samples = lax.optimization_barrier(blocked).astype(jnp.float32)
    tap_blocks = taps.reshape(tap_count, FIRST, second_len)

    def filtered(pieces, count):
        rows = []
        for spectrum in range(count):
            total = jnp.zeros((inputs, FIRST, second_len), jnp.float32)
            for offset in range(tap_count):
                total = total + tap_blocks[offset][None] * pieces[spectrum + offset]
            rows.append(total)
        return jnp.concatenate(rows, axis=0)

    scale = flags.astype(jnp.float32) / (8.0 * math.sqrt(length))
    groups_inp = lax.axis_size("inp")
    groups_tm = lax.axis_size("tm")
    count = float(groups_tm * spectra_dev * CH_AVG)

    def corner_turn(parts, count_s):
        spectra = (parts * jnp.tile(scale, count_s)[None, None, :, None]).astype(jnp.bfloat16)
        spectra = jnp.transpose(spectra, (1, 0, 2, 3))
        turned = lax.all_to_all(spectra, ("inp", "tm"), split_axis=0, concat_axis=0, tiled=True)
        own = turned.reshape(groups_inp, groups_tm, 2, count_s, inputs, FIRST)
        return own, lax.all_gather(own, "bl", axis=4, tiled=True)

    own_pieces = [samples[:, j] for j in range(spectra_dev)]
    keep = (lax.axis_index("tm") != 0).astype(jnp.float32)
    wrapped = [previous.astype(jnp.float32)] + [piece * keep for piece in own_pieces[:reach]]
    first_part = transform(filtered(own_pieces, 1), length, precision)
    own, gathered = corner_turn(first_part, 1)
    visibilities = correlate(own, gathered, None, 1.0 / count)
    next_pieces = [following[:, j].astype(jnp.float32) for j in range(ahead)]
    later = spectra_dev - 2
    rest = own_pieces[1:] + next_pieces
    second_part = jnp.concatenate(
        [transform(filtered(wrapped, 1), length, precision)]
        + [transform(filtered(rest[j:], 1), length, precision) for j in range(later)],
        axis=2,
    )
    own, gathered = corner_turn(second_part, later + 1)
    visibilities = correlate(own, gathered, visibilities, 1.0 / count)
    return visibilities.reshape(2, FIRST // CH_AVG, groups_inp, inputs, -1)


def solution(mesh):
    in_specs = (P(("inp", "bl"), "tm"), P(), P(("inp", "bl")))
    out_specs = P(None, ("inp", "tm"), None, "bl", None)
    return jax.shard_map(shards, mesh=mesh, in_specs=in_specs, out_specs=out_specs, check_vma=False)
```
